32 devices in a mesh: dp: 16 (over z, y, core), owner: 2 (over x).
Axes of the slice: x: 2, y: 2, z: 4, core: 2. Of those that a mesh axis runs over, the one named last changes fastest.
Arguments:
- inputs: bfloat16 [2048, 8192], P('dp'), may hold values from -8 to 8
- out_grads: bfloat16 [2048, 1024], P('dp', 'owner'), may hold values from -12 to 12
- weights: float32 [32, 512, 512], P(('dp', 'owner')), may hold values from -0.0625 to 0.0625
- left_stats: float32 [32, 512, 512], P(('dp', 'owner')), as said below
- right_stats: float32 [32, 512, 512], P(('dp', 'owner')), as said below
- left_roots: float32 [32, 512, 512], P(('dp', 'owner')), as said below
- right_roots: float32 [32, 512, 512], P(('dp', 'owner')), as said below
- refresh: int32 [32], P(('dp', 'owner')), may hold values from 0 to 1, as said below
Outputs:
- new_left_stats: float32 [32, 512, 512], P(('dp', 'owner'))
- new_right_stats: float32 [32, 512, 512], P(('dp', 'owner'))
- new_left_roots: float32 [32, 512, 512], P(('dp', 'owner'))
- new_right_roots: float32 [32, 512, 512], P(('dp', 'owner'))
- update: float32 [32, 512, 512], P(('dp', 'owner'))
- queries: bfloat16 [2048, 1024], P('dp', 'owner')
The draws below stay inside these ranges and needn't reach their ends.
Inputs may be any that keep to these rules, and one draw needn't show every extreme that they name: For every k, refresh[2k] + refresh[2k + 1] is at most 1, and refresh[0] + refresh[1] is 1. `left_stats`: every block is symmetric positive definite. `right_stats`: every block is symmetric positive definite. `left_roots`: every block is symmetric positive definite. `right_roots`: every block is symmetric positive definite.
All inputs are finite; a program needn't handle non-finite values.
Results may differ from the reference program's by a relative error of at most 0.015.
Values may be sent and summed in bfloat16 or wider, within the bound.
A program may use at most 128 MiB of HBM per device.

```python
import math
import jax
import jax.numpy as jnp
from jax import lax

D = 8192
B = 512
NEWTON = 2
TOKENS = 2048
COL_DEV = 512
COLS = 1024
BLOCKS = 32
N_DP = 16
N_OWNER = 2


def definite(key, count, order):
    keys = jax.random.split(key, 2)
    noise = jax.random.normal(keys[0], (count, order, order), jnp.float32) * (0.4 / order ** 0.5)
    noise = (noise + jnp.swapaxes(noise, 1, 2)) * 0.5 ** 0.5
    diagonal = jnp.exp(jax.random.uniform(keys[1], (count, order), jnp.float32, 0.0, 1.0986))
    identity = jnp.eye(order, dtype=jnp.float32)
    matrix = noise + diagonal[:, :, None] * identity[None, :, :]
    return matrix


def draw_left_stats(key, part):
    return definite(jax.random.fold_in(key, 11), BLOCKS, B)


def draw_right_stats(key, part):
    return definite(jax.random.fold_in(key, 12), BLOCKS, B)


def draw_left_roots(key, part):
    return definite(jax.random.fold_in(key, 13), BLOCKS, B)


def draw_right_roots(key, part):
    return definite(jax.random.fold_in(key, 14), BLOCKS, B)


def draw_refresh(key, part):
    pair_count = BLOCKS // 2
    keys = jax.random.split(jax.random.fold_in(key, 21), 2)
    active = (jax.random.randint(keys[0], (pair_count,), 0, 3) > 0).astype(jnp.int32)
    active = active.at[0].set(1)
    which_one = jax.random.randint(keys[1], (pair_count,), 0, 2)
    first_flag = active * (which_one == 0).astype(jnp.int32)
    second_flag = active - first_flag
    return jnp.stack([first_flag, second_flag], 1).reshape(BLOCKS)


def raised(entries, key, source, target, shards_of, factor):
    owner, partner = [(jnp.arange(entries.shape[position]) // (entries.shape[position] // shards_of)).reshape([-1 if axis == position else 1 for axis in range(entries.ndim)]) for position in (source, target)]
    chosen = jax.random.permutation(key, shards_of)[partner]
    strong = (owner == chosen) | (owner == (partner + shards_of // 2) % shards_of)
    return jnp.where(strong, factor * entries, entries)


def levels(own_key, shape, cuts, least, top_value):
    gain, own = 1.0, jax.random.fold_in(own_key, 6)
    for axis_at, shards_of in cuts:
        heights = jnp.exp(jax.random.uniform(jax.random.fold_in(own, axis_at), (shards_of,), jnp.float32, least / len(cuts), top_value / len(cuts)))
        gain = gain * jnp.repeat(heights, shape[axis_at] // shards_of).reshape([-1 if axis == axis_at else 1 for axis in range(len(shape))])
    return gain


def bell_draw(rng, extent, scale, bound, cuts=(), held_as=jnp.bfloat16):
    values = scale * jax.random.normal(rng, extent, jnp.float32)
    if cuts:
        values = values * levels(rng, extent, cuts, -0.22, 0.18)
    return jnp.clip(values, -bound, bound).astype(held_as)


def heavy_noise(rng, dims, scale, bound, shards, heavy, kind=jnp.bfloat16):
    drawn = scale * jax.random.normal(rng, dims, jnp.float32)
    if shards:
        drawn = drawn * levels(rng, dims, shards, -0.22, 0.18)
    return jnp.clip(raised(drawn, jax.random.fold_in(rng, 3), *heavy), -bound, bound).astype(kind)


def setup_inputs(seed: int = 0) -> dict:
    seeds = jax.random.split(jax.random.key(seed), 9)
    inputs = heavy_noise(seeds[0], (TOKENS, D), 1.0, 8.0, ((0, 16),), (0, 1, 16, 2.0))
    out_grads = bell_draw(seeds[1], (TOKENS, COLS), ((TOKENS / B) ** 0.5), 12.0, ((0, 16), (1, 2)))
    weights = bell_draw(seeds[2], (BLOCKS, B, B), D ** -0.5, 0.0625, ((0, 32),), jnp.float32)
    left_stats = draw_left_stats(jax.random.fold_in(seeds[8], 71), 0)
    right_stats = draw_right_stats(jax.random.fold_in(seeds[8], 71), 0)
    left_roots = draw_left_roots(jax.random.fold_in(seeds[8], 71), 0)
    right_roots = draw_right_roots(jax.random.fold_in(seeds[8], 71), 0)
    refresh = draw_refresh(jax.random.fold_in(seeds[8], 71), 0)
    return {"inputs": inputs, "out_grads": out_grads, "weights": weights, "left_stats": left_stats, "right_stats": right_stats, "left_roots": left_roots, "right_roots": right_roots, "refresh": refresh}


BETA = 0.95
DAMPING = 0.0001
HIGHEST = lax.Precision.HIGHEST

def matmul(left_mat, right_mat):
    return jnp.dot(left_mat, right_mat, precision=HIGHEST, preferred_element_type=jnp.float32)

def inverse_root(statistic):
    identity = jnp.eye(statistic.shape[0], dtype=jnp.float32)
    damped = statistic + DAMPING * identity
    factor_z = 2.5 / jnp.sqrt(jnp.sum(damped * damped))
    current = factor_z * damped
    result = jnp.sqrt(jnp.sqrt(factor_z)) * identity
    for turn in range(NEWTON):
        factor = 1.25 * identity - 0.25 * current
        result = matmul(result, factor)
        square = matmul(factor, factor)
        current = matmul(matmul(square, square), current)
    return result

def both_roots(left_stat, right_stat, left_old, right_old):
    return (inverse_root(left_stat), inverse_root(right_stat))

def stale_roots(left_stat, right_stat, left_old, right_old):
    return (left_old, right_old)

def reference(inputs, out_grads, weights, left_stats, right_stats, left_roots, right_roots, refresh):
    tok_total = inputs.shape[0]
    tok_local = tok_total // N_DP
    row_blocks = D // B
    col_blocks = COL_DEV // B
    x_parts = inputs.reshape(N_DP, tok_local, D)
    g_parts = out_grads.reshape(N_DP, tok_local, COLS)

    def add_part(running, pieces):
        x_piece, g_piece = pieces
        product = lax.dot_general(x_piece, g_piece, (((0,), (0,)), ((), ())), preferred_element_type=jnp.float32) / tok_total
        product = lax.optimization_barrier(product.astype(jnp.bfloat16))
        return (running + product.astype(jnp.float32), None)
    grad, unused = lax.scan(add_part, jnp.zeros((D, COLS), jnp.float32), (x_parts, g_parts))
    grad_blocks = grad.reshape(row_blocks, B, N_OWNER, col_blocks, B).transpose(0, 3, 2, 1, 4).reshape(BLOCKS, B, B)
    rate = 0.25 / math.sqrt(D)

    def per_block(items):
        grad_block, weight_block, left_stat, right_stat, left_old, right_old, flag_value = items
        left_new = BETA * left_stat + (1.0 - BETA) * matmul(grad_block, grad_block.T)
        right_new = BETA * right_stat + (1.0 - BETA) * matmul(grad_block.T, grad_block)
        left_root, right_root = lax.cond(flag_value > 0, both_roots, stale_roots, left_new, right_new, left_old, right_old)
        direction = matmul(matmul(left_root, grad_block), right_root)
        direction = direction * (B / jnp.sqrt(jnp.sum(direction * direction) + 1e-12))
        updated = (weight_block - rate * direction).astype(jnp.bfloat16)
        return (left_new, right_new, left_root, right_root, direction, updated)
    outputs = lax.map(per_block, (grad_blocks, weights, left_stats, right_stats, left_roots, right_roots, refresh))
    left_new, right_new, left_root, right_root, direction, updated = outputs
    full_weight = updated.reshape(row_blocks, col_blocks, N_OWNER, B, B).transpose(0, 3, 2, 1, 4).reshape(D, COLS)
    queries = jnp.dot(inputs, full_weight, preferred_element_type=jnp.float32).astype(jnp.bfloat16)
    return (left_new, right_new, left_root, right_root, direction, queries)
```

```python
import functools
import math

import jax
import jax.numpy as jnp
from jax import lax
from jax.experimental import pallas as pl
from jax.experimental.pallas import tpu as pltpu
from jax.sharding import PartitionSpec as P

BETA = 0.95
DAMPING = 0.0001
BF16 = jnp.bfloat16
F32 = jnp.float32


def dot(a, b, dims=((1,), (0,))):
    return lax.dot_general(a.astype(BF16), b.astype(BF16), (dims, ((), ())), preferred_element_type=F32)


def split(a):
    high = a.astype(BF16)
    return high, (a - high.astype(F32)).astype(BF16)


def dot3(a, b):
    a_high, a_low = split(a)
    b_high, b_low = split(b)
    return dot(a_high, b_high) + (dot(a_high, b_low) + dot(a_low, b_high))


def inverse_root(statistic):
    shape = statistic.shape
    eye = (lax.broadcasted_iota(jnp.int32, shape, 0) == lax.broadcasted_iota(jnp.int32, shape, 1)).astype(F32)
    damped = statistic + DAMPING * eye
    z = 2.5 / jnp.sqrt(jnp.sum(damped * damped, keepdims=True))
    m = z * damped
    p = dot(m, m)
    r = 1.5625 * m - 0.625 * p + 0.0625 * dot(p, m)
    w = 0.0625 * r + 0.1953125 * m - 0.01953125 * p
    return jnp.sqrt(jnp.sqrt(z)) * (1.5625 * eye - 0.3125 * m - 0.48828125 * r + dot(w, r))


def roots(left_stat, right_stat, left_old, right_old):
    return (inverse_root(left_stat), inverse_root(right_stat))


def stale(left_stat, right_stat, left_old, right_old):
    return (left_old, right_old)

LINE = 4


def flip(index, stride):
    return index + stride - 2 * stride * lax.rem(lax.div(index, stride), 2)


def remote(src, dst, send, recv, peer):
    return pltpu.make_async_remote_copy(
        src_ref=src, dst_ref=dst, send_sem=send, recv_sem=recv,
        device_id=peer, device_id_type=pl.DeviceIdType.MESH,
    )


def greet(peers):
    barrier = pltpu.get_barrier_semaphore()
    for peer in peers:
        pl.semaphore_signal(barrier, inc=1, device_id=peer, device_id_type=pl.DeviceIdType.MESH)
    pl.semaphore_wait(barrier, len(peers))


def toggle(index, bits):
    stride = 1
    while stride <= bits:
        if bits & stride:
            index = flip(index, stride)
        stride *= 2
    return index


ORDER = (
    "g", "x1", "x10", "x2", "x14", "x3", "x4", "h", "x6", "x11", "x15", "x5", "x8", "x7", "x12", "x9",
    "x13", "i1", "p1", "p2", "p4", "p10", "y0", "p3", "i3", "p14", "p6", "p11", "y2", "p15", "d0", "p5",
    "p7", "y1", "d2", "p8", "p12", "d10", "p9", "p13", "y3", "d14", "s3", "s11", "s15", "d6", "s7", "d4",
    "s5", "d8", "s9", "d12", "s13",
)


class Copies:
    def __init__(self):
        self.sent = []

    def go(self, src, dst, send, recv, peer):
        copy = remote(src, dst, send, recv, peer)
        copy.start()
        self.sent.append(copy)
        return copy

    def drain(self):
        for copy in self.sent:
            copy.wait_send()


def gather_phase(n, copies, x_ref, g_ref, f, fs, ga, grad, own, x_s, x_r, p_s, p_r, z_s, z_r, y_s, y_r, c_s, c_r, s_s, s_r):
    me, mine = lax.axis_index("dp"), lax.axis_index("owner")
    rows, width = g_ref.shape
    half = rows // 2
    near = pl.ds(pl.multiple_of(mine * half, half), half)
    pair, row = flip(me, 1), flip(me, 2)
    go = copies.go

    def cols(block):
        return pl.ds(pl.multiple_of(block * width, width), width)

    own_in = [
        pltpu.make_async_copy(x_ref.at[:, cols(me)], f.at[me], own.at[0]),
        pltpu.make_async_copy(g_ref, ga.at[me], own.at[1]),
        pltpu.make_async_copy(x_ref.at[:, cols(pair)], fs.at[lax.div(me, 2)], own.at[2]),
    ]
    x_copy, p_copy, z_copy, y_copy, c_copy, s_copy = {}, {}, {}, {}, {}, {}

    def fan(t, block):
        slot = toggle(me, LINE * t)
        y_copy[t] = go(block, ga.at[slot], y_s.at[t], y_r.at[t], (row, mine))
        c_copy[t] = go(block, ga.at[slot], c_s.at[t], c_r.at[t], (pair, mine))

    def g(_):
        for copy in own_in:
            copy.start()
        for t in (2, 1):
            z_copy[t] = go(g_ref, ga.at[me], z_s.at[t], z_r.at[t], (toggle(me, LINE * t), mine))
        fan(0, g_ref)

    def h(_):
        z_copy[2].wait_recv()
        held = ga.at[toggle(me, LINE * 2)]
        z_copy[3] = go(held, held, z_s.at[3], z_r.at[3], (toggle(me, LINE), mine))
        fan(2, held)

    def i(t):
        z_copy[t].wait_recv()
        fan(t, ga.at[toggle(me, LINE * t)])

    def y(t):
        y_copy[t].wait_recv()
        held = ga.at[toggle(row, LINE * t)]
        c_copy[LINE + t] = go(held, held, c_s.at[LINE + t], c_r.at[LINE + t], (pair, mine))

    def x(k):
        peer = toggle(me, k)
        if k == 1:
            src, dst = x_ref.at[:, cols(peer)], f.at[me]
        else:
            src, dst = x_ref.at[near, cols(peer)], f.at[me, near]
        x_copy[k] = go(src, dst, x_s.at[k], x_r.at[k], (peer, mine))

    def p(k):
        x_copy[k].wait_recv()
        if k > 1:
            held = f.at[toggle(me, k), near]
            p_copy[k] = go(held, held, p_s.at[k], p_r.at[k], (me, 1 - mine))

    def d(k):
        for at in (k, k + 1):
            if at > 1:
                p_copy[at].wait_recv()
        if k == 0:
            own_in[0].wait()
            own_in[1].wait()
        t = k // LINE
        c_copy[t + LINE if k % LINE else t].wait_recv()
        chip = pl.multiple_of(2 * lax.div(toggle(me, k), 2), 2)
        term = dot(
            f[pl.ds(chip, 2)].reshape(2 * rows, width), ga[pl.ds(chip, 2)].reshape(2 * rows, width), ((0,), (0,))
        )
        grad[...] = term if k == 0 else grad[...] + term

    def s(k):
        source = toggle(me, k)
        s_copy[k] = go(f.at[source], fs.at[lax.div(source, 2)], s_s.at[k], s_r.at[k], (pair, mine))

    steps = dict(g=g, h=h, i=i, y=y, x=x, p=p, d=d, s=s)
    for word in ORDER:
        steps[word[0]](int(word[1:] or 0))
    return own_in[2], s_copy


def reduce_phase(n, copies, f, fs, u, us, arrived, tot, a_out, a_in, b_out, b_in, a_s, a_r, b_s, b_r, u_copy, q_ref):
    me, mine = lax.axis_index("dp"), lax.axis_index("owner")
    row = flip(me, 2)
    rows = q_ref.shape[0]
    half = rows // 2
    go = copies.go
    halves = [pl.ds(k * half, half) for k in range(2)]

    def near_part(base, t):
        return dot(f[toggle(base, LINE * t)], u[...])

    def far_part(base, t):
        return dot(fs[lax.div(toggle(base, LINE * t), 2)], us[...])

    a_copy, b_copy = {}, {}
    ahead = near_part(row, 3)
    for copy in arrived:
        copy.wait()
    for copy in u_copy:
        copy.wait_recv()
    for t in (3, 2, 1, 0):
        a_out[t] = ((ahead if t == 3 else near_part(row, t)) + far_part(row, t)).astype(BF16)
        for k in range(2):
            a_copy[t, k] = go(a_out.at[t, halves[k]], a_in.at[t, halves[k]], a_s.at[2 * t + k], a_r.at[2 * t + k], (row, mine))

    def total(t):
        tot[t] = near_part(me, t) + far_part(me, t)

    def pass_on(t, k, peer, extra=None):
        a_copy[t, k].wait_recv()
        value = tot[t, halves[k]] + a_in[t, halves[k]].astype(F32)
        if extra is not None:
            b_copy[extra, k].wait_recv()
            value = value + b_in[extra, halves[k]].astype(F32)
        b_out[t, halves[k]] = value.astype(BF16)
        b_copy[t, k] = go(b_out.at[t, halves[k]], b_in.at[t, halves[k]], b_s.at[2 * t + k], b_r.at[2 * t + k], (peer, mine))

    total(3)
    for k in range(2):
        pass_on(3, k, toggle(me, LINE))
    total(2)
    total(1)
    total(0)
    for k in range(2):
        pass_on(2, k, toggle(me, 2 * LINE), 3)
    for k in range(2):
        pass_on(1, k, toggle(me, LINE))
    for k in range(2):
        a_copy[0, k].wait_recv()
        value = tot[0, halves[k]] + a_in[0, halves[k]].astype(F32)
        b_copy[2, k].wait_recv()
        value = value + b_in[2, halves[k]].astype(F32)
        b_copy[1, k].wait_recv()
        q_ref[halves[k]] = (value + b_in[1, halves[k]].astype(F32)).astype(BF16)


def step_kernel(n, rate, flag, x_ref, g_ref, w_hbm, ls_hbm, rs_hbm, lr_hbm, rr_hbm,
                ls_out, rs_out, lr_out, rr_out, d_out, q_ref,
                f, fs, ga, grad, w, ls, rs, lr, rr, d, u, us, tot, a_out, a_in, b_out, b_in,
                in_sem, out_sem, own, x_s, x_r, p_s, p_r, z_s, z_r, y_s, y_r, c_s, c_r, s_s, s_r, u_s, u_r, a_s, a_r, b_s, b_r):
    me, mine = lax.axis_index("dp"), lax.axis_index("owner")
    pair = flip(me, 1)
    block = w.shape[0]
    greet([(toggle(me, k), mine) for k in range(1, n)] + [(me, 1 - mine)])
    copies = Copies()
    ins = [
        pltpu.make_async_copy(src.at[0], dst, in_sem.at[k])
        for k, (src, dst) in enumerate(((ls_hbm, ls), (rs_hbm, rs), (lr_hbm, lr), (rr_hbm, rr), (w_hbm, w)))
    ]
    for copy in ins:
        copy.start()
    own_side, s_copy = gather_phase(
        n, copies, x_ref, g_ref, f, fs, ga, grad, own, x_s, x_r, p_s, p_r, z_s, z_r, y_s, y_r, c_s, c_r, s_s, s_r
    )
    outs = [
        pltpu.make_async_copy(src, dst.at[0], out_sem.at[k])
        for k, (src, dst) in enumerate(((ls, ls_out), (rs, rs_out), (lr, lr_out), (rr, rr_out), (d, d_out)))
    ]
    grad[...] = grad[...] * (1.0 / (n * g_ref.shape[0]))
    high = grad[...].astype(BF16)
    for copy in ins:
        copy.wait()
    ls[...] = BETA * ls[...] + (1.0 - BETA) * dot(high, high, ((1,), (1,)))
    outs[0].start()
    rs[...] = BETA * rs[...] + (1.0 - BETA) * dot(high, high, ((0,), (0,)))
    outs[1].start()
    anew = jnp.full((block, block), flag[0], jnp.int32) > 0
    lr[...] = jnp.where(anew, inverse_root(ls[...]), lr[...])
    outs[2].start()
    rr[...] = jnp.where(anew, inverse_root(rs[...]), rr[...])
    outs[3].start()
    direction = dot3(dot3(lr[...], grad[...]), rr[...])
    norm = jnp.sqrt(jnp.sum(direction * direction, keepdims=True) + 1e-12)
    direction = direction * (block / norm)
    d[...] = direction
    outs[4].start()
    u[...] = (w[...] - rate * direction).astype(BF16)
    u_copy = [copies.go(u, us, u_s.at[0], u_r.at[0], (pair, mine))]
    for copy in s_copy.values():
        copy.wait_recv()
    reduce_phase(n, copies, f, fs, u, us, [own_side], tot, a_out, a_in, b_out, b_in, a_s, a_r, b_s, b_r, u_copy, q_ref)
    for copy in outs:
        copy.wait()
    copies.drain()


def fused_step(n, rate, inputs, out_grads, weights, left_stats, right_stats, left_roots, right_roots, refresh):
    rows, width = out_grads.shape
    block = weights.shape[1]
    nz = n // LINE
    dma = pltpu.SemaphoreType.DMA
    anywhere = pl.BlockSpec(memory_space=pl.ANY)
    square = pltpu.VMEM((block, block), F32)
    narrow = pltpu.VMEM((block, block), BF16)
    shards = pltpu.VMEM((nz, rows, width), BF16)
    return pl.pallas_call(
        functools.partial(step_kernel, n, rate),
        out_shape=[jax.ShapeDtypeStruct((1, block, block), F32)] * 5 + [jax.ShapeDtypeStruct((rows, width), BF16)],
        in_specs=[pl.BlockSpec(memory_space=pltpu.SMEM)] + [anywhere] * 7,
        out_specs=[anywhere] * 5 + [pl.BlockSpec(memory_space=pltpu.VMEM)],
        scratch_shapes=[
            pltpu.VMEM((n, rows, block), BF16), pltpu.VMEM((n // 2, rows, block), BF16), pltpu.VMEM((n, rows, width), BF16),
        ] + [square] * 7 + [narrow] * 2 + [pltpu.VMEM((nz, rows, width), F32)] + [shards] * 4
        + [dma((5,))] * 2 + [dma((3,))] + [dma((n,))] * 4 + [dma((LINE,))] * 4 + [dma((2 * LINE,))] * 2 + [dma((n,))] * 2
        + [dma((1,))] * 2 + [dma((2 * LINE,))] * 4,
        compiler_params=pltpu.CompilerParams(collective_id=0, has_side_effects=True, vmem_limit_bytes=48 << 20),
        name="fused_step",
    )(refresh, inputs, out_grads, weights, left_stats, right_stats, left_roots, right_roots)


def body(inputs, out_grads, weights, left_stats, right_stats, left_roots, right_roots, refresh):
    tok_local, model_width = inputs.shape
    block = weights.shape[1]
    col_count = out_grads.shape[1]
    row_blocks = model_width // block
    col_blocks = col_count // block
    replicas = lax.axis_size("dp")
    tok_total = tok_local * replicas
    kernels = col_blocks == 1 and lax.axis_size("owner") == 2 and replicas == 4 * LINE
    rate = 0.25 / math.sqrt(model_width)
    if kernels:
        return fused_step(
            replicas, rate, inputs, out_grads, weights, left_stats, right_stats, left_roots, right_roots, refresh
        )
    mine = lax.axis_index("dp") % col_blocks
    grads = lax.all_gather(out_grads, "dp", axis=0, tiled=True)
    grads = lax.dynamic_slice_in_dim(grads, mine * block, block, 1)
    send = jnp.repeat(inputs.reshape(tok_local, row_blocks, block).transpose(1, 0, 2), col_blocks, axis=0)
    features = lax.all_to_all(send, "dp", split_axis=0, concat_axis=0, tiled=True)
    features = features.reshape(tok_total, block)
    gradient = dot(features, grads, ((0,), (0,))) / tok_total
    left_new = BETA * left_stats[0] + (1.0 - BETA) * dot(gradient, gradient, ((1,), (1,)))
    right_new = BETA * right_stats[0] + (1.0 - BETA) * dot(gradient, gradient, ((0,), (0,)))
    left_root, right_root = lax.cond(
        refresh[0] > 0, roots, stale, left_new, right_new, left_roots[0], right_roots[0]
    )
    direction = dot3(dot3(left_root, gradient), right_root)
    direction = direction * (block / jnp.sqrt(jnp.sum(direction * direction) + 1e-12))
    updated = (weights[0] - rate * direction).astype(BF16)
    partial = dot(features, updated).astype(BF16)
    if col_blocks > 1:
        partial = lax.dynamic_update_slice(jnp.zeros((tok_total, col_count), BF16), partial, (0, mine * block))
    queries = lax.psum_scatter(partial, "dp", scatter_dimension=0, tiled=True)
    return (left_new[None], right_new[None], left_root[None], right_root[None], direction[None], queries)


def solution(mesh):
    blocks = P(("dp", "owner"), None, None)
    in_specs = (P("dp", None), P("dp", "owner"), blocks, blocks, blocks, blocks, blocks, P(("dp", "owner")))
    out_specs = (blocks,) * 5 + (P("dp", "owner"),)
    return jax.shard_map(body, mesh=mesh, in_specs=in_specs, out_specs=out_specs, check_vma=False)
```

```python
import functools
import math

import jax
import jax.numpy as jnp
from jax import lax
from jax.experimental import pallas as pl
from jax.experimental.pallas import tpu as pltpu
from jax.sharding import PartitionSpec as P

BETA = 0.95
DAMPING = 0.0001
BF16 = jnp.bfloat16
F32 = jnp.float32


def dot(a, b, dims=((1,), (0,))):
    return lax.dot_general(a.astype(BF16), b.astype(BF16), (dims, ((), ())), preferred_element_type=F32)


def split(a):
    high = a.astype(BF16)
    return high, (a - high.astype(F32)).astype(BF16)


def dot3(a, b):
    a_high, a_low = split(a)
    b_high, b_low = split(b)
    return dot(a_high, b_high) + (dot(a_high, b_low) + dot(a_low, b_high))


def inverse_roots(*statistics):
    shape = statistics[0].shape
    eye = (lax.broadcasted_iota(jnp.int32, shape, 0) == lax.broadcasted_iota(jnp.int32, shape, 1)).astype(F32)
    damped = [s + DAMPING * eye for s in statistics]
    z = [2.5 / jnp.sqrt(jnp.sum(a * a, keepdims=True)) for a in damped]
    m = [scale * a for scale, a in zip(z, damped)]
    p = [dot(a, a) for a in m]
    q = [dot(b, a) for a, b in zip(m, p)]
    r = [1.5625 * a - 0.625 * b + 0.0625 * c for a, b, c in zip(m, p, q)]
    w = [0.0625 * c + 0.1953125 * a - 0.01953125 * b for a, b, c in zip(m, p, r)]
    last = [dot(a, b) for a, b in zip(w, r)]
    return tuple(
        jnp.sqrt(jnp.sqrt(scale)) * (1.5625 * eye - 0.3125 * a - 0.48828125 * b + c)
        for scale, a, b, c in zip(z, m, r, last)
    )


def roots(left_stat, right_stat, left_old, right_old):
    return inverse_roots(left_stat, right_stat)


def stale(left_stat, right_stat, left_old, right_old):
    return (left_old, right_old)

LINE = 4


def flip(index, stride):
    return index + stride - 2 * stride * lax.rem(lax.div(index, stride), 2)


def remote(src, dst, send, recv, peer):
    return pltpu.make_async_remote_copy(
        src_ref=src, dst_ref=dst, send_sem=send, recv_sem=recv,
        device_id=peer, device_id_type=pl.DeviceIdType.MESH,
    )


def greet(peers):
    barrier = pltpu.get_barrier_semaphore()
    for peer in peers:
        pl.semaphore_signal(barrier, inc=1, device_id=peer, device_id_type=pl.DeviceIdType.MESH)
    pl.semaphore_wait(barrier, len(peers))


def toggle(index, bits):
    stride = 1
    while stride <= bits:
        if bits & stride:
            index = flip(index, stride)
        stride *= 2
    return index


ORDER = (
    "g", "x1", "x10", "x2", "x14", "x3", "x4", "h", "x6", "x11", "x15", "x5", "x8", "x7", "x12", "x9",
    "x13", "i1", "p1", "p2", "p4", "p10", "y0", "p3", "i3", "p14", "p6", "p11", "y2", "p15", "d0", "p5",
    "p7", "y1", "d2", "p8", "p12", "d10", "p9", "p13", "y3", "d14", "s3", "s11", "s15", "d6", "s7", "d4",
    "s5", "d8", "s9", "d12", "s13",
)


class Copies:
    def __init__(self):
        self.sent = []

    def go(self, src, dst, send, recv, peer):
        copy = remote(src, dst, send, recv, peer)
        copy.start()
        self.sent.append(copy)
        return copy

    def drain(self):
        for copy in self.sent:
            copy.wait_send()


def gather_phase(n, copies, x_ref, g_ref, f, fs, ga, grad, own, x_s, x_r, p_s, p_r, z_s, z_r, y_s, y_r, c_s, c_r, s_s, s_r):
    me, mine = lax.axis_index("dp"), lax.axis_index("owner")
    rows, width = g_ref.shape
    half = rows // 2
    near = pl.ds(pl.multiple_of(mine * half, half), half)
    pair, row = flip(me, 1), flip(me, 2)
    go = copies.go

    def cols(block):
        return pl.ds(pl.multiple_of(block * width, width), width)

    own_in = [
        pltpu.make_async_copy(x_ref.at[:, cols(me)], f.at[me], own.at[0]),
        pltpu.make_async_copy(g_ref, ga.at[me], own.at[1]),
        pltpu.make_async_copy(x_ref.at[:, cols(pair)], fs.at[lax.div(me, 2)], own.at[2]),
    ]
    x_copy, p_copy, z_copy, y_copy, c_copy, s_copy = {}, {}, {}, {}, {}, {}

    def fan(t, block):
        slot = toggle(me, LINE * t)
        y_copy[t] = go(block, ga.at[slot], y_s.at[t], y_r.at[t], (row, mine))
        c_copy[t] = go(block, ga.at[slot], c_s.at[t], c_r.at[t], (pair, mine))

    def g(_):
        for copy in own_in:
            copy.start()
        for t in (2, 1):
            z_copy[t] = go(g_ref, ga.at[me], z_s.at[t], z_r.at[t], (toggle(me, LINE * t), mine))
        fan(0, g_ref)

    def h(_):
        z_copy[2].wait_recv()
        held = ga.at[toggle(me, LINE * 2)]
        z_copy[3] = go(held, held, z_s.at[3], z_r.at[3], (toggle(me, LINE), mine))
        fan(2, held)

    def i(t):
        z_copy[t].wait_recv()
        fan(t, ga.at[toggle(me, LINE * t)])

    def y(t):
        y_copy[t].wait_recv()
        held = ga.at[toggle(row, LINE * t)]
        c_copy[LINE + t] = go(held, held, c_s.at[LINE + t], c_r.at[LINE + t], (pair, mine))

    def x(k):
        peer = toggle(me, k)
        if k == 1:
            src, dst = x_ref.at[:, cols(peer)], f.at[me]
        else:
            src, dst = x_ref.at[near, cols(peer)], f.at[me, near]
        x_copy[k] = go(src, dst, x_s.at[k], x_r.at[k], (peer, mine))

    def p(k):
        x_copy[k].wait_recv()
        if k > 1:
            held = f.at[toggle(me, k), near]
            p_copy[k] = go(held, held, p_s.at[k], p_r.at[k], (me, 1 - mine))

    def d(k):
        for at in (k, k + 1):
            if at > 1:
                p_copy[at].wait_recv()
        if k == 0:
            own_in[0].wait()
            own_in[1].wait()
        t = k // LINE
        c_copy[t + LINE if k % LINE else t].wait_recv()
        chip = pl.multiple_of(2 * lax.div(toggle(me, k), 2), 2)
        term = dot(
            f[pl.ds(chip, 2)].reshape(2 * rows, width), ga[pl.ds(chip, 2)].reshape(2 * rows, width), ((0,), (0,))
        )
        grad[...] = term if k == 0 else grad[...] + term

    def s(k):
        source = toggle(me, k)
        s_copy[k] = go(f.at[source], fs.at[lax.div(source, 2)], s_s.at[k], s_r.at[k], (pair, mine))

    steps = dict(g=g, h=h, i=i, y=y, x=x, p=p, d=d, s=s)
    for word in ORDER:
        with jax.named_scope(word):
            steps[word[0]](int(word[1:] or 0))
    return own_in[2], s_copy


def reduce_phase(n, copies, f, fs, u, us, arrived, tot, a_out, a_in, b_out, b_in, a_s, a_r, b_s, b_r, u_copy, q_ref):
    me, mine = lax.axis_index("dp"), lax.axis_index("owner")
    row = flip(me, 2)
    rows = q_ref.shape[0]
    half = rows // 2
    go = copies.go
    halves = [pl.ds(k * half, half) for k in range(2)]

    def near_part(base, t):
        return dot(f[toggle(base, LINE * t)], u[...])

    def far_part(base, t):
        return dot(fs[lax.div(toggle(base, LINE * t), 2)], us[...])

    a_copy, b_copy = {}, {}
    ahead = near_part(row, 3)
    with jax.named_scope("swap"):
        for copy in arrived:
            copy.wait()
        for copy in u_copy:
            copy.wait_recv()

    def offer(t):
        part = (ahead if t == 3 else near_part(row, t)) + far_part(row, t)
        a_out[t] = part.astype(BF16)
        for k in range(2):
            a_copy[t, k] = go(a_out.at[t, halves[k]], a_in.at[t, halves[k]], a_s.at[2 * t + k], a_r.at[2 * t + k], (row, mine))

    def total(t):
        tot[t] = near_part(me, t) + far_part(me, t)

    def pass_on(t, k, peer, extra=None):
        a_copy[t, k].wait_recv()
        value = tot[t, halves[k]] + a_in[t, halves[k]].astype(F32)
        if extra is not None:
            b_copy[extra, k].wait_recv()
            value = value + b_in[extra, halves[k]].astype(F32)
        b_out[t, halves[k]] = value.astype(BF16)
        b_copy[t, k] = go(b_out.at[t, halves[k]], b_in.at[t, halves[k]], b_s.at[2 * t + k], b_r.at[2 * t + k], (peer, mine))

    for t in (3, 2, 1, 0):
        with jax.named_scope(f"offer{t}"):
            offer(t)
    with jax.named_scope("total3"):
        total(3)
    for k in range(2):
        with jax.named_scope(f"pass3{k}"):
            pass_on(3, k, toggle(me, LINE))
    for t in (2, 1, 0):
        with jax.named_scope(f"total{t}"):
            total(t)
    for k in range(2):
        with jax.named_scope(f"pass2{k}"):
            pass_on(2, k, toggle(me, 2 * LINE), 3)
    for k in range(2):
        with jax.named_scope(f"pass1{k}"):
            pass_on(1, k, toggle(me, LINE))
    for k in range(2):
        with jax.named_scope(f"last{k}"):
            a_copy[0, k].wait_recv()
            value = tot[0, halves[k]] + a_in[0, halves[k]].astype(F32)
            b_copy[2, k].wait_recv()
            value = value + b_in[2, halves[k]].astype(F32)
            b_copy[1, k].wait_recv()
            q_ref[halves[k]] = (value + b_in[1, halves[k]].astype(F32)).astype(BF16)


def step_kernel(n, rate, flag, x_ref, g_ref, w_hbm, ls_hbm, rs_hbm, lr_hbm, rr_hbm,
                ls_out, rs_out, lr_out, rr_out, d_out, q_ref,
                f, fs, ga, grad, w, ls, rs, lr, rr, d, u, us, q, tot, a_out, a_in, b_out, b_in,
                in_sem, out_sem, own, x_s, x_r, p_s, p_r, z_s, z_r, y_s, y_r, c_s, c_r, s_s, s_r, u_s, u_r, a_s, a_r, b_s, b_r):
    me, mine = lax.axis_index("dp"), lax.axis_index("owner")
    pair = flip(me, 1)
    block = w.shape[0]
    with jax.named_scope("greet"):
        greet([(toggle(me, k), mine) for k in range(1, n)] + [(me, 1 - mine)])
    copies = Copies()
    ins = [
        pltpu.make_async_copy(src.at[0], dst, in_sem.at[k])
        for k, (src, dst) in enumerate(((ls_hbm, ls), (rs_hbm, rs), (lr_hbm, lr), (rr_hbm, rr), (w_hbm, w)))
    ]
    for copy in ins:
        copy.start()
    own_side, s_copy = gather_phase(
        n, copies, x_ref, g_ref, f, fs, ga, grad, own, x_s, x_r, p_s, p_r, z_s, z_r, y_s, y_r, c_s, c_r, s_s, s_r
    )
    outs = [
        pltpu.make_async_copy(src, dst.at[0], out_sem.at[k])
        for k, (src, dst) in enumerate(((ls, ls_out), (rs, rs_out), (lr, lr_out), (rr, rr_out), (d, d_out)))
    ]
    with jax.named_scope("stats"):
        for copy in ins:
            copy.wait()
        high = (grad[...] * (1.0 / (n * g_ref.shape[0]))).astype(BF16)
        ls[...] = BETA * ls[...] + (1.0 - BETA) * dot(high, high, ((1,), (1,)))
        rs[...] = BETA * rs[...] + (1.0 - BETA) * dot(high, high, ((0,), (0,)))
        outs[0].start()
        outs[1].start()
    with jax.named_scope("roots"):
        anew = jnp.full((block, block), flag[0], jnp.int32) > 0
        left, right = inverse_roots(ls[...], rs[...])
        lr[...] = jnp.where(anew, left, lr[...])
        rr[...] = jnp.where(anew, right, rr[...])
        outs[2].start()
        outs[3].start()
    with jax.named_scope("direction"):
        d[...] = dot(dot(lr[...], high), rr[...])
    with jax.named_scope("update"):
        direction = d[...]
        scale = block / jnp.sqrt(jnp.sum(direction * direction, keepdims=True) + 1e-12)
    u_copy = []
    for k in range(2):
        with jax.named_scope(f"weights{k}"):
            part = pl.ds(k * block // 2, block // 2)
            u[part] = (w[part] - (rate * scale) * d[part]).astype(BF16)
            u_copy.append(copies.go(u.at[part], us.at[part], u_s.at[k], u_r.at[k], (pair, mine)))
    with jax.named_scope("scaled"):
        d[...] = scale * d[...]
        outs[4].start()
    for copy in s_copy.values():
        copy.wait_recv()
    reduce_phase(n, copies, f, fs, u, us, [own_side], tot, a_out, a_in, b_out, b_in, a_s, a_r, b_s, b_r, u_copy, q)
    with jax.named_scope("drain"):
        q_out = pltpu.make_async_copy(q, q_ref, out_sem.at[5])
        q_out.start()
        q_out.wait()
        for copy in outs:
            copy.wait()
        copies.drain()


def fused_step(n, rate, inputs, out_grads, weights, left_stats, right_stats, left_roots, right_roots, refresh):
    rows, width = out_grads.shape
    block = weights.shape[1]
    nz = n // LINE
    dma = pltpu.SemaphoreType.DMA
    anywhere = pl.BlockSpec(memory_space=pl.ANY)
    square = pltpu.VMEM((block, block), F32)
    narrow = pltpu.VMEM((block, block), BF16)
    shards = pltpu.VMEM((nz, rows, width), BF16)
    return pl.pallas_call(
        functools.partial(step_kernel, n, rate),
        out_shape=[jax.ShapeDtypeStruct((1, block, block), F32)] * 5 + [jax.ShapeDtypeStruct((rows, width), BF16)],
        in_specs=[pl.BlockSpec(memory_space=pltpu.SMEM)] + [pl.BlockSpec(memory_space=pltpu.HBM)] * 7,
        out_specs=[anywhere] * 6,
        scratch_shapes=[
            pltpu.VMEM((n, rows, block), BF16), pltpu.VMEM((n // 2, rows, block), BF16), pltpu.VMEM((n, rows, width), BF16),
        ] + [square] * 7 + [narrow] * 2 + [pltpu.VMEM((rows, width), BF16)] + [pltpu.VMEM((nz, rows, width), F32)] + [shards] * 4
        + [dma((5,)), dma((6,)), dma((3,))] + [dma((n,))] * 4 + [dma((LINE,))] * 4 + [dma((2 * LINE,))] * 2 + [dma((n,))] * 2
        + [dma((2,))] * 2 + [dma((2 * LINE,))] * 4,
        compiler_params=pltpu.CompilerParams(collective_id=0, has_side_effects=True, vmem_limit_bytes=48 << 20),
        name="fused_step",
    )(refresh, inputs, pltpu.with_memory_space_constraint(out_grads, pltpu.HBM), weights, left_stats, right_stats, left_roots, right_roots)


def hand_out_kernel(*refs):
    count = len(refs) // 2
    copies = [pltpu.make_async_copy(refs[k], refs[count + k], refs[-1].at[k]) for k in range(count)]
    for copy in copies:
        copy.start()
    for copy in copies:
        copy.wait()


def hand_out(*arrays):
    anywhere = pl.BlockSpec(memory_space=pl.ANY)
    return pl.pallas_call(
        hand_out_kernel,
        out_shape=[jax.ShapeDtypeStruct(a.shape, a.dtype) for a in arrays],
        in_specs=[anywhere] * len(arrays),
        out_specs=[pl.BlockSpec(memory_space=pltpu.HBM)] * len(arrays),
        scratch_shapes=[pltpu.SemaphoreType.DMA((len(arrays),))],
        compiler_params=pltpu.CompilerParams(vmem_limit_bytes=1 << 20),
        name="hand_out",
    )(*arrays)


def body(inputs, out_grads, weights, left_stats, right_stats, left_roots, right_roots, refresh):
    tok_local, model_width = inputs.shape
    block = weights.shape[1]
    col_count = out_grads.shape[1]
    row_blocks = model_width // block
    col_blocks = col_count // block
    replicas = lax.axis_size("dp")
    tok_total = tok_local * replicas
    kernels = col_blocks == 1 and lax.axis_size("owner") == 2 and replicas == 4 * LINE
    rate = 0.25 / math.sqrt(model_width)
    if kernels:
        return hand_out(*fused_step(
            replicas, rate, inputs, out_grads, weights, left_stats, right_stats, left_roots, right_roots, refresh
        ))
    mine = lax.axis_index("dp") % col_blocks
    grads = lax.all_gather(out_grads, "dp", axis=0, tiled=True)
    grads = lax.dynamic_slice_in_dim(grads, mine * block, block, 1)
    send = jnp.repeat(inputs.reshape(tok_local, row_blocks, block).transpose(1, 0, 2), col_blocks, axis=0)
    features = lax.all_to_all(send, "dp", split_axis=0, concat_axis=0, tiled=True)
    features = features.reshape(tok_total, block)
    gradient = dot(features, grads, ((0,), (0,))) / tok_total
    left_new = BETA * left_stats[0] + (1.0 - BETA) * dot(gradient, gradient, ((1,), (1,)))
    right_new = BETA * right_stats[0] + (1.0 - BETA) * dot(gradient, gradient, ((0,), (0,)))
    left_root, right_root = lax.cond(
        refresh[0] > 0, roots, stale, left_new, right_new, left_roots[0], right_roots[0]
    )
    direction = dot3(dot3(left_root, gradient), right_root)
    direction = direction * (block / jnp.sqrt(jnp.sum(direction * direction) + 1e-12))
    updated = (weights[0] - rate * direction).astype(BF16)
    partial = dot(features, updated).astype(BF16)
    if col_blocks > 1:
        partial = lax.dynamic_update_slice(jnp.zeros((tok_total, col_count), BF16), partial, (0, mine * block))
    queries = lax.psum_scatter(partial, "dp", scatter_dimension=0, tiled=True)
    return (left_new[None], right_new[None], left_root[None], right_root[None], direction[None], queries)


def solution(mesh):
    blocks = P(("dp", "owner"), None, None)
    in_specs = (P("dp", None), P("dp", "owner"), blocks, blocks, blocks, blocks, blocks, P(("dp", "owner")))
    out_specs = (blocks,) * 5 + (P("dp", "owner"),)
    return jax.shard_map(body, mesh=mesh, in_specs=in_specs, out_specs=out_specs, check_vma=False)
```

```python
import functools
import math

import jax
import jax.numpy as jnp
from jax import lax
from jax.experimental import pallas as pl
from jax.experimental.pallas import tpu as pltpu
from jax.sharding import PartitionSpec as P

BETA = 0.95
DAMPING = 0.0001
BF16 = jnp.bfloat16
F32 = jnp.float32


def dot(a, b, dims=((1,), (0,))):
    return lax.dot_general(a.astype(BF16), b.astype(BF16), (dims, ((), ())), preferred_element_type=F32)


def split(a):
    high = a.astype(BF16)
    return high, (a - high.astype(F32)).astype(BF16)


def dot3(a, b):
    a_high, a_low = split(a)
    b_high, b_low = split(b)
    return dot(a_high, b_high) + (dot(a_high, b_low) + dot(a_low, b_high))


def inverse_roots(*statistics):
    shape = statistics[0].shape
    eye = (lax.broadcasted_iota(jnp.int32, shape, 0) == lax.broadcasted_iota(jnp.int32, shape, 1)).astype(F32)
    damped = [s + DAMPING * eye for s in statistics]
    z = [2.5 / jnp.sqrt(jnp.sum(a * a, keepdims=True)) for a in damped]
    m = [scale * a for scale, a in zip(z, damped)]
    p = [dot(a, a) for a in m]
    q = [dot(b, a) for a, b in zip(m, p)]
    r = [1.5625 * a - 0.625 * b + 0.0625 * c for a, b, c in zip(m, p, q)]
    w = [0.0625 * c + 0.1953125 * a - 0.01953125 * b for a, b, c in zip(m, p, r)]
    last = [dot(a, b) for a, b in zip(w, r)]
    return tuple(
        jnp.sqrt(jnp.sqrt(scale)) * (1.5625 * eye - 0.3125 * a - 0.48828125 * b + c)
        for scale, a, b, c in zip(z, m, r, last)
    )


def roots(left_stat, right_stat, left_old, right_old):
    return inverse_roots(left_stat, right_stat)


def stale(left_stat, right_stat, left_old, right_old):
    return (left_old, right_old)

LINE = 4


def flip(index, stride):
    return index + stride - 2 * stride * lax.rem(lax.div(index, stride), 2)


def remote(src, dst, send, recv, peer):
    return pltpu.make_async_remote_copy(
        src_ref=src, dst_ref=dst, send_sem=send, recv_sem=recv,
        device_id=peer, device_id_type=pl.DeviceIdType.MESH,
    )


def greet(peers):
    barrier = pltpu.get_barrier_semaphore()
    for peer in peers:
        pl.semaphore_signal(barrier, inc=1, device_id=peer, device_id_type=pl.DeviceIdType.MESH)
    pl.semaphore_wait(barrier, len(peers))


def toggle(index, bits):
    stride = 1
    while stride <= bits:
        if bits & stride:
            index = flip(index, stride)
        stride *= 2
    return index


ORDER = (
    "g", "x1", "x10", "x2", "x14", "x3", "x4", "h", "x6", "x11", "x15", "x5", "x8", "x7", "x12", "x9",
    "x13", "i1", "p1", "p2", "p4", "p10", "y0", "p3", "i3", "p14", "p6", "p11", "y2", "p15", "d0", "p5",
    "p7", "y1", "d2", "p8", "p12", "d10", "p9", "p13", "y3", "d14", "s3", "s11", "s15", "d6", "s7", "d4",
    "s5", "d8", "s9", "d12", "s13",
)


PARTS = {9: 2, 13: 2}
EXTRA = {(9, 1): 0, (13, 1): 16}


def landed(view, sem):
    pltpu.make_async_copy(view, view, sem).wait()


class Copies:
    def __init__(self, send):
        self.send = send

    def group(self, at):
        def go(src, dst, recv, peer):
            copy = remote(src, dst, self.send.at[at], recv, peer)
            copy.start()
            return copy

        return go


def gather_phase(n, copies, x_ref, g_ref, f, fs, ga, grad, own, x_r, p_r, z_r, y_r, c_r, s_r):
    me, mine = lax.axis_index("dp"), lax.axis_index("owner")
    rows, width = g_ref.shape
    half = rows // 2
    far = pl.ds(pl.multiple_of((1 - mine) * half, half), half)
    pair, row = flip(me, 1), flip(me, 2)
    go_x, go_g, go_s = copies.group(0), copies.group(1), copies.group(2)

    def cols(block):
        return pl.ds(pl.multiple_of(block * width, width), width)

    own_in = [
        pltpu.make_async_copy(x_ref.at[:, cols(me)], f.at[me], own.at[0]),
        pltpu.make_async_copy(g_ref, ga.at[me], own.at[1]),
        pltpu.make_async_copy(x_ref.at[:, cols(pair)], fs.at[lax.div(me, 2)], own.at[2]),
    ]
    x_copy, z_copy, y_copy, c_copy = {}, {}, {}, {}

    def fan(t, block):
        slot = toggle(me, LINE * t)
        y_copy[t] = go_g(block, ga.at[slot], y_r.at[t], (row, mine))
        c_copy[t] = go_g(block, ga.at[slot], c_r.at[t], (pair, mine))

    def g(_):
        for copy in own_in:
            copy.start()
        for t in (2, 1):
            z_copy[t] = go_g(g_ref, ga.at[me], z_r.at[t], (toggle(me, LINE * t), mine))
        fan(0, g_ref)

    def h(_):
        z_copy[2].wait_recv()
        held = ga.at[toggle(me, LINE * 2)]
        z_copy[3] = go_g(held, held, z_r.at[3], (toggle(me, LINE), mine))
        fan(2, held)

    def i(t):
        z_copy[t].wait_recv()
        fan(t, ga.at[toggle(me, LINE * t)])

    def y(t):
        y_copy[t].wait_recv()
        held = ga.at[toggle(row, LINE * t)]
        c_copy[LINE + t] = go_g(held, held, c_r.at[LINE + t], (pair, mine))

    def slices(k):
        count = PARTS.get(k, 1)
        span = half // count
        return [pl.ds(pl.multiple_of(mine * half + at * span, span), span) for at in range(count)]

    def x(k):
        peer = toggle(me, k)
        if k == 1:
            x_copy[k] = [go_x(x_ref.at[:, cols(peer)], f.at[me], x_r.at[k], (peer, mine))]
            return
        x_copy[k] = []
        for at, part in enumerate(slices(k)):
            sem = x_r.at[k if at == 0 else EXTRA[k, at]]
            x_copy[k].append(go_x(x_ref.at[part, cols(peer)], f.at[me, part], sem, (peer, mine)))

    def p(k):
        if k == 1:
            x_copy[k][0].wait_recv()
            return
        for at, part in enumerate(slices(k)):
            x_copy[k][at].wait_recv()
            held = f.at[toggle(me, k), part]
            go_x(held, held, p_r.at[k // 2], (me, 1 - mine))

    def d(k):
        chip = pl.ds(pl.multiple_of(2 * lax.div(toggle(me, k), 2), 2), 2)
        if k:
            landed(f.at[chip, far], p_r.at[k // 2])
        else:
            own_in[0].wait()
            own_in[1].wait()
        t = k // LINE
        c_copy[t + LINE if k % LINE else t].wait_recv()
        term = dot(f[chip].reshape(2 * rows, width), ga[chip].reshape(2 * rows, width), ((0,), (0,)))
        grad[...] = term if k == 0 else grad[...] + term

    def s(k):
        source = toggle(me, k)
        go_s(f.at[source], fs.at[lax.div(source, 2)], s_r.at[0], (pair, mine))

    steps = dict(g=g, h=h, i=i, y=y, x=x, p=p, d=d, s=s)
    for word in ORDER:
        with jax.named_scope(word):
            steps[word[0]](int(word[1:] or 0))
    return own_in[2]


def reduce_phase(copies, f, fs, u, us, arrive, q, tot, keep, a_out, a_in, b_out, b_in, e_out, e_in, h_out, h_in, g_out, g_in,
                 a_r, b_r, e_r):
    me, mine = lax.axis_index("dp"), lax.axis_index("owner")
    row = flip(me, 2)
    rows = q.shape[0]
    cut = rows // 4
    half = (rows - cut) // 2
    go = copies.group(3)
    first = pl.ds(0, cut)
    rest = [pl.ds(cut + k * half, half) for k in range(2)]
    spans = [pl.ds(k * half, half) for k in range(2)]
    near_z, far_z, across = (toggle(me, LINE), mine), (toggle(me, 2 * LINE), mine), (row, mine)

    def near_part(base, t):
        return dot(f[toggle(base, LINE * t)], u[...])

    def far_part(base, t):
        return dot(fs[lax.div(toggle(base, LINE * t), 2)], us[...])

    a_copy, b_copy = {}, {}
    ahead = near_part(row, 3)
    with jax.named_scope("swap"):
        arrive()

    def part(base, t):
        return near_part(base, t) + far_part(base, t)

    def early(k, value):
        e_out[k] = value[:cut].astype(BF16)
        go(e_out.at[k], e_in.at[k], e_r.at[k // 2], near_z)

    def stage(t, value):
        a_out[t] = value[cut:].astype(BF16)

    def offer(t, k):
        a_copy[t, k] = go(a_out.at[t, spans[k]], a_in.at[t, spans[k]], a_r.at[2 * t + k], across)

    def pass_on(t, k, peer, extra=None):
        a_copy[t, k].wait_recv()
        value = tot[t, rest[k]] + a_in[t, spans[k]].astype(F32)
        if extra is not None:
            b_copy[extra, k].wait_recv()
            value = value + b_in[extra, spans[k]].astype(F32)
        b_out[t, spans[k]] = value.astype(BF16)
        b_copy[t, k] = go(b_out.at[t, spans[k]], b_in.at[t, spans[k]], b_r.at[2 * t + k], peer)

    with jax.named_scope("offer3"):
        value = ahead + far_part(row, 3)
        stage(3, value)
        offer(3, 0)
        offer(3, 1)
        early(0, value)
    with jax.named_scope("offer1"):
        value = part(row, 1)
        early(1, value)
        stage(1, value)
    with jax.named_scope("total3"):
        value = part(me, 3)
        early(2, value)
        tot[3] = value
    with jax.named_scope("offer2"):
        value = part(row, 2)
        stage(2, value)
        offer(2, 0)
        offer(2, 1)
        keep[0] = value[:cut]
    with jax.named_scope("total1"):
        value = part(me, 1)
        early(3, value)
        tot[1] = value
    with jax.named_scope("offer0"):
        value = part(row, 0)
        stage(0, value)
        keep[1] = value[:cut]
    with jax.named_scope("pass30"):
        pass_on(3, 0, near_z)
    with jax.named_scope("total2"):
        tot[2] = part(me, 2)
    with jax.named_scope("pass31"):
        pass_on(3, 1, near_z)
    with jax.named_scope("hop"):
        landed(e_in.at[pl.ds(0, 2)], e_r.at[0])
        h_copy = []
        for k in range(2):
            h_out[k] = (keep[k] + e_in[k].astype(F32)).astype(BF16)
            h_copy.append(go(h_out.at[k], h_in.at[k], e_r.at[3 + k], across))
    for t in (1, 0):
        offer(t, 0)
        offer(t, 1)
    with jax.named_scope("total0"):
        tot[0] = part(me, 0)
    for k in range(2):
        with jax.named_scope(f"pass2{k}"):
            pass_on(2, k, far_z, 3)
    with jax.named_scope("hand"):
        landed(e_in.at[pl.ds(2, 2)], e_r.at[1])
        h_copy[0].wait_recv()
        g_out[...] = (tot[2, first] + e_in[2].astype(F32) + h_in[0].astype(F32)).astype(BF16)
        g_copy = go(g_out, g_in, e_r.at[2], far_z)
    with jax.named_scope("pass10"):
        pass_on(1, 0, near_z)
    with jax.named_scope("pass11"):
        pass_on(1, 1, near_z)
    with jax.named_scope("first"):
        h_copy[1].wait_recv()
        g_copy.wait_recv()
        q[first] = (tot[0, first] + e_in[3].astype(F32) + h_in[1].astype(F32) + g_in[...].astype(F32)).astype(BF16)
    for k in range(2):
        with jax.named_scope(f"last{k}"):
            a_copy[0, k].wait_recv()
            value = tot[0, rest[k]] + a_in[0, spans[k]].astype(F32)
            for t in (2, 1):
                b_copy[t, k].wait_recv()
                value = value + b_in[t, spans[k]].astype(F32)
            q[rest[k]] = value.astype(BF16)


def step_kernel(n, rate, flag, x_ref, g_ref, w_hbm, ls_hbm, rs_hbm, lr_hbm, rr_hbm,
                ls_out, rs_out, lr_out, rr_out, d_out, q_ref,
                f, fs, ga, grad, w, ls, rs, lr, rr, d, u, us, q, tot, keep, a_out, a_in, b_out, b_in, e_out, e_in, h_out, h_in, g_out, g_in,
                in_sem, out_sem, send, own, x_r, p_r, z_r, y_r, c_r, s_r, u_r, a_r, b_r, e_r):
    me, mine = lax.axis_index("dp"), lax.axis_index("owner")
    pair = flip(me, 1)
    block = w.shape[0]
    with jax.named_scope("greet"):
        greet([(toggle(me, k), mine) for k in range(1, n)] + [(me, 1 - mine)])
    copies = Copies(send)
    ins = [
        pltpu.make_async_copy(src.at[0], dst, in_sem.at[k])
        for k, (src, dst) in enumerate(((ls_hbm, ls), (rs_hbm, rs), (lr_hbm, lr), (rr_hbm, rr), (w_hbm, w)))
    ]
    for copy in ins:
        copy.start()
    own_side = gather_phase(n, copies, x_ref, g_ref, f, fs, ga, grad, own, x_r, p_r, z_r, y_r, c_r, s_r)
    outs = [
        pltpu.make_async_copy(src, dst.at[0], out_sem.at[k])
        for k, (src, dst) in enumerate(((ls, ls_out), (rs, rs_out), (lr, lr_out), (rr, rr_out), (d, d_out)))
    ]
    with jax.named_scope("stats"):
        for copy in ins:
            copy.wait()
        high = (grad[...] * (1.0 / (n * g_ref.shape[0]))).astype(BF16)
        ls[...] = BETA * ls[...] + (1.0 - BETA) * dot(high, high, ((1,), (1,)))
        rs[...] = BETA * rs[...] + (1.0 - BETA) * dot(high, high, ((0,), (0,)))
        outs[0].start()
        outs[1].start()
    with jax.named_scope("roots"):
        anew = jnp.full((block, block), flag[0], jnp.int32) > 0
        left, right = inverse_roots(ls[...], rs[...])
        lr[...] = jnp.where(anew, left, lr[...])
        rr[...] = jnp.where(anew, right, rr[...])
        outs[2].start()
        outs[3].start()
    with jax.named_scope("direction"):
        d[...] = dot(dot(lr[...], high), rr[...])
    with jax.named_scope("update"):
        direction = d[...]
        scale = block / jnp.sqrt(jnp.sum(direction * direction, keepdims=True) + 1e-12)
    for k in range(2):
        with jax.named_scope(f"weights{k}"):
            part = pl.ds(k * block // 2, block // 2)
            u[part] = (w[part] - (rate * scale) * d[part]).astype(BF16)
            copies.group(2)(u.at[part], us.at[part], u_r.at[0], (pair, mine))
    with jax.named_scope("scaled"):
        d[...] = scale * d[...]
        outs[4].start()

    def arrive():
        own_side.wait()
        landed(fs.at[pl.ds(0, n // 2 - 1)], s_r.at[0])
        landed(us, u_r.at[0])

    reduce_phase(
        copies, f, fs, u, us, arrive, q, tot, keep,
        a_out, a_in, b_out, b_in, e_out, e_in, h_out, h_in, g_out, g_in, a_r, b_r, e_r,
    )
    with jax.named_scope("drain"):
        q_out = pltpu.make_async_copy(q, q_ref, out_sem.at[5])
        q_out.start()
        q_out.wait()
        for copy in outs:
            copy.wait()
        for at, units in enumerate((n - 1, n - 1, n // 2 + 3, n // 2 - 1)):
            landed(f.at[pl.ds(0, units)], send.at[at])


def fused_step(n, rate, inputs, out_grads, weights, left_stats, right_stats, left_roots, right_roots, refresh):
    rows, width = out_grads.shape
    block = weights.shape[1]
    nz = n // LINE
    dma = pltpu.SemaphoreType.DMA
    anywhere = pl.BlockSpec(memory_space=pl.ANY)
    square = pltpu.VMEM((block, block), F32)
    narrow = pltpu.VMEM((block, block), BF16)
    cut = rows // 4
    shards = pltpu.VMEM((nz, rows - cut, width), BF16)
    return pl.pallas_call(
        functools.partial(step_kernel, n, rate),
        out_shape=[jax.ShapeDtypeStruct((1, block, block), F32)] * 5 + [jax.ShapeDtypeStruct((rows, width), BF16)],
        in_specs=[pl.BlockSpec(memory_space=pltpu.SMEM)] + [pl.BlockSpec(memory_space=pltpu.HBM)] * 7,
        out_specs=[anywhere] * 6,
        scratch_shapes=[
            pltpu.VMEM((n, rows, block), BF16), pltpu.VMEM((n // 2, rows, block), BF16), pltpu.VMEM((n, rows, width), BF16),
        ] + [square] * 7 + [narrow] * 2 + [pltpu.VMEM((rows, width), BF16)] + [pltpu.VMEM((nz, rows, width), F32), pltpu.VMEM((2, cut, width), F32)] + [shards] * 4
        + [pltpu.VMEM((4, cut, width), BF16)] * 2 + [pltpu.VMEM((2, cut, width), BF16)] * 2 + [pltpu.VMEM((cut, width), BF16)] * 2
        + [dma((5,)), dma((6,)), dma((4,)), dma((3,))]
        + [dma((n + len(EXTRA) - 1,)), dma((n // 2,)), dma((LINE,)), dma((LINE,)), dma((2 * LINE,)), dma((1,)), dma((1,))]
        + [dma((2 * LINE,)), dma((2 * LINE,)), dma((5,))],
        compiler_params=pltpu.CompilerParams(collective_id=0, has_side_effects=True, vmem_limit_bytes=48 << 20),
        name="fused_step",
    )(refresh, inputs, pltpu.with_memory_space_constraint(out_grads, pltpu.HBM), weights, left_stats, right_stats, left_roots, right_roots)


def hand_out_kernel(*refs):
    count = len(refs) // 2
    copies = [pltpu.make_async_copy(refs[k], refs[count + k], refs[-1].at[k]) for k in range(count)]
    for copy in copies:
        copy.start()
    for copy in copies:
        copy.wait()


def hand_out(*arrays):
    anywhere = pl.BlockSpec(memory_space=pl.ANY)
    return pl.pallas_call(
        hand_out_kernel,
        out_shape=[jax.ShapeDtypeStruct(a.shape, a.dtype) for a in arrays],
        in_specs=[anywhere] * len(arrays),
        out_specs=[pl.BlockSpec(memory_space=pltpu.HBM)] * len(arrays),
        scratch_shapes=[pltpu.SemaphoreType.DMA((len(arrays),))],
        compiler_params=pltpu.CompilerParams(vmem_limit_bytes=1 << 20),
        name="hand_out",
    )(*arrays)


def body(inputs, out_grads, weights, left_stats, right_stats, left_roots, right_roots, refresh):
    tok_local, model_width = inputs.shape
    block = weights.shape[1]
    col_count = out_grads.shape[1]
    row_blocks = model_width // block
    col_blocks = col_count // block
    replicas = lax.axis_size("dp")
    tok_total = tok_local * replicas
    kernels = col_blocks == 1 and lax.axis_size("owner") == 2 and replicas == 4 * LINE and block == 4 * tok_local
    rate = 0.25 / math.sqrt(model_width)
    if kernels:
        return hand_out(*fused_step(
            replicas, rate, inputs, out_grads, weights, left_stats, right_stats, left_roots, right_roots, refresh
        ))
    mine = lax.axis_index("dp") % col_blocks
    grads = lax.all_gather(out_grads, "dp", axis=0, tiled=True)
    grads = lax.dynamic_slice_in_dim(grads, mine * block, block, 1)
    send = jnp.repeat(inputs.reshape(tok_local, row_blocks, block).transpose(1, 0, 2), col_blocks, axis=0)
    features = lax.all_to_all(send, "dp", split_axis=0, concat_axis=0, tiled=True)
    features = features.reshape(tok_total, block)
    gradient = dot(features, grads, ((0,), (0,))) / tok_total
    left_new = BETA * left_stats[0] + (1.0 - BETA) * dot(gradient, gradient, ((1,), (1,)))
    right_new = BETA * right_stats[0] + (1.0 - BETA) * dot(gradient, gradient, ((0,), (0,)))
    left_root, right_root = lax.cond(
        refresh[0] > 0, roots, stale, left_new, right_new, left_roots[0], right_roots[0]
    )
    direction = dot3(dot3(left_root, gradient), right_root)
    direction = direction * (block / jnp.sqrt(jnp.sum(direction * direction) + 1e-12))
    updated = (weights[0] - rate * direction).astype(BF16)
    partial = dot(features, updated).astype(BF16)
    if col_blocks > 1:
        partial = lax.dynamic_update_slice(jnp.zeros((tok_total, col_count), BF16), partial, (0, mine * block))
    queries = lax.psum_scatter(partial, "dp", scatter_dimension=0, tiled=True)
    return (left_new[None], right_new[None], left_root[None], right_root[None], direction[None], queries)


def solution(mesh):
    blocks = P(("dp", "owner"), None, None)
    in_specs = (P("dp", None), P("dp", "owner"), blocks, blocks, blocks, blocks, blocks, P(("dp", "owner")))
    out_specs = (blocks,) * 5 + (P("dp", "owner"),)
    return jax.shard_map(body, mesh=mesh, in_specs=in_specs, out_specs=out_specs, check_vma=False)
```

```python
import functools
import math

import jax
import jax.numpy as jnp
from jax import lax
from jax.experimental import pallas as pl
from jax.experimental.pallas import tpu as pltpu
from jax.sharding import PartitionSpec as P

BETA = 0.95
DAMPING = 0.0001
BF16 = jnp.bfloat16
F32 = jnp.float32


def dot(a, b, dims=((1,), (0,))):
    return lax.dot_general(a.astype(BF16), b.astype(BF16), (dims, ((), ())), preferred_element_type=F32)


def split(a):
    high = a.astype(BF16)
    return high, (a - high.astype(F32)).astype(BF16)


def dot3(a, b):
    a_high, a_low = split(a)
    b_high, b_low = split(b)
    return dot(a_high, b_high) + (dot(a_high, b_low) + dot(a_low, b_high))


def even_dot(a, b, dims=((1,), (0,))):
    half = a.shape[0] // 2
    a, b = a.astype(BF16), b.astype(BF16)

    def cut(x, axis, low):
        return (x[:half] if low else x[half:]) if axis == 0 else (x[:, :half] if low else x[:, half:])

    over, under = (cut(a, 1 - dims[0][0], low) for low in (True, False))
    upper = dot(over, b, dims)
    corner = dot(under, cut(b, 1 - dims[1][0], False), dims)
    return jnp.concatenate([upper, jnp.concatenate([upper[:, half:].T, corner], axis=1)], axis=0)


def inverse_roots(*statistics):
    shape = statistics[0].shape
    eye = (lax.broadcasted_iota(jnp.int32, shape, 0) == lax.broadcasted_iota(jnp.int32, shape, 1)).astype(F32)
    damped = [s + DAMPING * eye for s in statistics]
    squares = [even_dot(a, a) for a in damped]
    z = [2.5 / jnp.sqrt(jnp.sum(a * a, keepdims=True)) for a in damped]
    m = [scale * a for scale, a in zip(z, damped)]
    p = [(scale * scale) * a for scale, a in zip(z, squares)]
    q = [even_dot(b, a) for a, b in zip(m, p)]
    r = [1.5625 * a - 0.625 * b + 0.0625 * c for a, b, c in zip(m, p, q)]
    w = [0.0625 * c + 0.1953125 * a - 0.01953125 * b for a, b, c in zip(m, p, r)]
    last = [even_dot(a, b) for a, b in zip(w, r)]
    return tuple(
        jnp.sqrt(jnp.sqrt(scale)) * (1.5625 * eye - 0.3125 * a - 0.48828125 * b + c)
        for scale, a, b, c in zip(z, m, r, last)
    )


def roots(left_stat, right_stat, left_old, right_old):
    return inverse_roots(left_stat, right_stat)


def stale(left_stat, right_stat, left_old, right_old):
    return (left_old, right_old)

LINE = 4


def flip(index, stride):
    return index + stride - 2 * stride * lax.rem(lax.div(index, stride), 2)


def remote(src, dst, send, recv, peer):
    return pltpu.make_async_remote_copy(
        src_ref=src, dst_ref=dst, send_sem=send, recv_sem=recv,
        device_id=peer, device_id_type=pl.DeviceIdType.MESH,
    )


def greet(peers):
    barrier = pltpu.get_barrier_semaphore()
    for peer in peers:
        pl.semaphore_signal(barrier, inc=1, device_id=peer, device_id_type=pl.DeviceIdType.MESH)
    pl.semaphore_wait(barrier, len(peers))


def toggle(index, bits):
    stride = 1
    while stride <= bits:
        if bits & stride:
            index = flip(index, stride)
        stride *= 2
    return index


ORDER = (
    "g", "x1", "x10", "x2", "x14", "x3", "x4", "h", "x6", "x11", "x15", "x5", "x8", "x7", "x12", "x9",
    "x13", "i1", "p1", "p2", "p4", "p10", "y0", "p3", "i3", "p14", "p6", "p11", "y2", "p15", "d0", "p5",
    "p7", "y1", "d2", "p8", "p12", "d10", "p9", "p13", "y3", "d14", "s3", "s11", "s15", "d6", "s7", "d4",
    "s5", "d8", "s9", "d12", "s13",
)


PARTS = {9: 2, 13: 2}
EXTRA = {(9, 1): 0, (13, 1): 16}


def landed(view, sem):
    pltpu.make_async_copy(view, view, sem).wait()


class Copies:
    def __init__(self, send):
        self.send = send

    def group(self, at):
        def go(src, dst, recv, peer):
            copy = remote(src, dst, self.send.at[at], recv, peer)
            copy.start()
            return copy

        return go


def gather_phase(n, copies, x_ref, g_ref, f, fs, ga, grad, own, x_r, p_r, z_r, y_r, c_r, s_r):
    me, mine = lax.axis_index("dp"), lax.axis_index("owner")
    rows, width = g_ref.shape
    half = rows // 2
    far = pl.ds(pl.multiple_of((1 - mine) * half, half), half)
    pair, row = flip(me, 1), flip(me, 2)
    go_x, go_g, go_s = copies.group(0), copies.group(1), copies.group(2)

    def cols(block):
        return pl.ds(pl.multiple_of(block * width, width), width)

    own_in = [
        pltpu.make_async_copy(x_ref.at[:, cols(me)], f.at[me], own.at[0]),
        pltpu.make_async_copy(g_ref, ga.at[me], own.at[1]),
        pltpu.make_async_copy(x_ref.at[:, cols(pair)], fs.at[lax.div(me, 2)], own.at[2]),
    ]
    x_copy, z_copy, y_copy, c_copy = {}, {}, {}, {}

    def fan(t, block):
        slot = toggle(me, LINE * t)
        y_copy[t] = go_g(block, ga.at[slot], y_r.at[t], (row, mine))
        c_copy[t] = go_g(block, ga.at[slot], c_r.at[t], (pair, mine))

    def g(_):
        for copy in own_in:
            copy.start()
        for t in (2, 1):
            z_copy[t] = go_g(g_ref, ga.at[me], z_r.at[t], (toggle(me, LINE * t), mine))
        fan(0, g_ref)

    def h(_):
        z_copy[2].wait_recv()
        held = ga.at[toggle(me, LINE * 2)]
        z_copy[3] = go_g(held, held, z_r.at[3], (toggle(me, LINE), mine))
        fan(2, held)

    def i(t):
        z_copy[t].wait_recv()
        fan(t, ga.at[toggle(me, LINE * t)])

    def y(t):
        y_copy[t].wait_recv()
        held = ga.at[toggle(row, LINE * t)]
        c_copy[LINE + t] = go_g(held, held, c_r.at[LINE + t], (pair, mine))

    def slices(k):
        count = PARTS.get(k, 1)
        span = half // count
        return [pl.ds(pl.multiple_of(mine * half + at * span, span), span) for at in range(count)]

    def x(k):
        peer = toggle(me, k)
        if k == 1:
            x_copy[k] = [go_x(x_ref.at[:, cols(peer)], f.at[me], x_r.at[k], (peer, mine))]
            return
        x_copy[k] = []
        for at, part in enumerate(slices(k)):
            sem = x_r.at[k if at == 0 else EXTRA[k, at]]
            x_copy[k].append(go_x(x_ref.at[part, cols(peer)], f.at[me, part], sem, (peer, mine)))

    def p(k):
        if k == 1:
            x_copy[k][0].wait_recv()
            return
        for at, part in enumerate(slices(k)):
            x_copy[k][at].wait_recv()
            held = f.at[toggle(me, k), part]
            go_x(held, held, p_r.at[k // 2], (me, 1 - mine))

    def d(k):
        chip = pl.ds(pl.multiple_of(2 * lax.div(toggle(me, k), 2), 2), 2)
        if k:
            landed(f.at[chip, far], p_r.at[k // 2])
        else:
            own_in[0].wait()
            own_in[1].wait()
        t = k // LINE
        c_copy[t + LINE if k % LINE else t].wait_recv()
        term = dot(f[chip].reshape(2 * rows, width), ga[chip].reshape(2 * rows, width), ((0,), (0,)))
        grad[...] = term if k == 0 else grad[...] + term

    def s(k):
        source = toggle(me, k)
        go_s(f.at[source], fs.at[lax.div(source, 2)], s_r.at[0], (pair, mine))

    steps = dict(g=g, h=h, i=i, y=y, x=x, p=p, d=d, s=s)
    for word in ORDER:
        with jax.named_scope(word):
            steps[word[0]](int(word[1:] or 0))
    return own_in[2]


def reduce_phase(copies, f, fs, u, us, arrive, q, tot, keep, a_out, a_in, b_out, b_in, e_out, e_in, h_out, h_in, g_out, g_in,
                 a_r, b_r, e_r):
    me, mine = lax.axis_index("dp"), lax.axis_index("owner")
    row = flip(me, 2)
    rows = q.shape[0]
    cut = rows // 4
    half = (rows - cut) // 2
    go = copies.group(3)
    first = pl.ds(0, cut)
    rest = [pl.ds(cut + k * half, half) for k in range(2)]
    spans = [pl.ds(k * half, half) for k in range(2)]
    near_z, far_z, across = (toggle(me, LINE), mine), (toggle(me, 2 * LINE), mine), (row, mine)

    def near_part(base, t):
        return dot(f[toggle(base, LINE * t)], u[...])

    def far_part(base, t):
        return dot(fs[lax.div(toggle(base, LINE * t), 2)], us[...])

    a_copy, b_copy = {}, {}
    ahead = near_part(row, 3)
    with jax.named_scope("swap"):
        arrive()

    def part(base, t):
        return near_part(base, t) + far_part(base, t)

    def early(k, value):
        e_out[k] = value[:cut].astype(BF16)
        go(e_out.at[k], e_in.at[k], e_r.at[k // 2], near_z)

    def stage(t, value):
        a_out[t] = value[cut:].astype(BF16)

    def offer(t, k):
        a_copy[t, k] = go(a_out.at[t, spans[k]], a_in.at[t, spans[k]], a_r.at[2 * t + k], across)

    def pass_on(t, k, peer, extra=None):
        a_copy[t, k].wait_recv()
        value = tot[t, rest[k]] + a_in[t, spans[k]].astype(F32)
        if extra is not None:
            b_copy[extra, k].wait_recv()
            value = value + b_in[extra, spans[k]].astype(F32)
        b_out[t, spans[k]] = value.astype(BF16)
        b_copy[t, k] = go(b_out.at[t, spans[k]], b_in.at[t, spans[k]], b_r.at[2 * t + k], peer)

    with jax.named_scope("offer3"):
        value = ahead + far_part(row, 3)
        stage(3, value)
        offer(3, 0)
        offer(3, 1)
        early(0, value)
    with jax.named_scope("offer1"):
        value = part(row, 1)
        early(1, value)
        stage(1, value)
    with jax.named_scope("total3"):
        value = part(me, 3)
        early(2, value)
        tot[3] = value
    with jax.named_scope("offer2"):
        value = part(row, 2)
        stage(2, value)
        offer(2, 0)
        offer(2, 1)
        keep[0] = value[:cut]
    with jax.named_scope("total1"):
        value = part(me, 1)
        early(3, value)
        tot[1] = value
    with jax.named_scope("offer0"):
        value = part(row, 0)
        stage(0, value)
        keep[1] = value[:cut]
    with jax.named_scope("pass30"):
        pass_on(3, 0, (toggle(me, 3 * LINE), mine))
    with jax.named_scope("total2"):
        tot[2] = part(me, 2)
    with jax.named_scope("pass31"):
        pass_on(3, 1, near_z)
    with jax.named_scope("hop"):
        landed(e_in.at[pl.ds(0, 2)], e_r.at[0])
        h_copy = []
        for k in range(2):
            h_out[k] = (keep[k] + e_in[k].astype(F32)).astype(BF16)
            h_copy.append(go(h_out.at[k], h_in.at[k], e_r.at[3 + k], across))
    for t in (1, 0):
        offer(t, 0)
        offer(t, 1)
    with jax.named_scope("total0"):
        tot[0] = part(me, 0)
    for k in range(2):
        with jax.named_scope(f"pass2{k}"):
            pass_on(2, k, far_z, 3 if k else None)
    with jax.named_scope("hand"):
        landed(e_in.at[pl.ds(2, 2)], e_r.at[1])
        h_copy[0].wait_recv()
        g_out[...] = (tot[2, first] + e_in[2].astype(F32) + h_in[0].astype(F32)).astype(BF16)
        g_copy = go(g_out, g_in, e_r.at[2], far_z)
    with jax.named_scope("pass10"):
        pass_on(1, 0, near_z)
    with jax.named_scope("pass11"):
        pass_on(1, 1, near_z)
    with jax.named_scope("first"):
        h_copy[1].wait_recv()
        g_copy.wait_recv()
        q[first] = (tot[0, first] + e_in[3].astype(F32) + h_in[1].astype(F32) + g_in[...].astype(F32)).astype(BF16)
    for k in range(2):
        with jax.named_scope(f"last{k}"):
            a_copy[0, k].wait_recv()
            value = tot[0, rest[k]] + a_in[0, spans[k]].astype(F32)
            for t in (2, 1) if k else (3, 2, 1):
                b_copy[t, k].wait_recv()
                value = value + b_in[t, spans[k]].astype(F32)
            q[rest[k]] = value.astype(BF16)


def step_kernel(n, rate, flag, x_ref, g_ref, w_hbm, ls_hbm, rs_hbm, lr_hbm, rr_hbm,
                ls_out, rs_out, lr_out, rr_out, d_out, q_ref,
                f, fs, ga, grad, w, ls, rs, lr, rr, d, u, us, q, tot, keep, a_out, a_in, b_out, b_in, e_out, e_in, h_out, h_in, g_out, g_in,
                in_sem, out_sem, send, own, x_r, p_r, z_r, y_r, c_r, s_r, u_r, a_r, b_r, e_r):
    me, mine = lax.axis_index("dp"), lax.axis_index("owner")
    pair = flip(me, 1)
    block = w.shape[0]
    with jax.named_scope("greet"):
        greet([(toggle(me, k), mine) for k in range(1, n)] + [(me, 1 - mine)])
    copies = Copies(send)
    ins = [
        pltpu.make_async_copy(src.at[0], dst, in_sem.at[k])
        for k, (src, dst) in enumerate(((ls_hbm, ls), (rs_hbm, rs), (lr_hbm, lr), (rr_hbm, rr), (w_hbm, w)))
    ]
    for copy in ins:
        copy.start()
    own_side = gather_phase(n, copies, x_ref, g_ref, f, fs, ga, grad, own, x_r, p_r, z_r, y_r, c_r, s_r)
    outs = [
        pltpu.make_async_copy(src, dst.at[0], out_sem.at[k])
        for k, (src, dst) in enumerate(((ls, ls_out), (rs, rs_out), (lr, lr_out), (rr, rr_out), (d, d_out)))
    ]
    with jax.named_scope("stats"):
        for copy in ins:
            copy.wait()
        high = (grad[...] * (1.0 / (n * g_ref.shape[0]))).astype(BF16)
        ls[...] = BETA * ls[...] + (1.0 - BETA) * even_dot(high, high, ((1,), (1,)))
        rs[...] = BETA * rs[...] + (1.0 - BETA) * even_dot(high, high, ((0,), (0,)))
        outs[0].start()
        outs[1].start()
    with jax.named_scope("roots"):
        anew = jnp.full((block, block), flag[0], jnp.int32) > 0
        left, right = inverse_roots(ls[...], rs[...])
        lr[...] = jnp.where(anew, left, lr[...])
        rr[...] = jnp.where(anew, right, rr[...])
        outs[2].start()
        outs[3].start()
    with jax.named_scope("direction"):
        through = dot(lr[...], high).astype(BF16)
        last = rr[...].astype(BF16)
        total = jnp.zeros((8, block), F32)
        for k in range(4):
            span = block // 4
            value = dot(through[k * span : (k + 1) * span], last)
            d[pl.ds(k * span, span)] = value
            total = total + jnp.sum((value * value).reshape(span // 8, 8, block), axis=0)
    with jax.named_scope("update"):
        scale = block / jnp.sqrt(jnp.sum(total, keepdims=True) + 1e-12)
    for k in range(2):
        with jax.named_scope(f"weights{k}"):
            part = pl.ds(k * block // 2, block // 2)
            u[part] = (w[part] - (rate * scale) * d[part]).astype(BF16)
            copies.group(2)(u.at[part], us.at[part], u_r.at[0], (pair, mine))
    with jax.named_scope("scaled"):
        d[...] = scale * d[...]
        outs[4].start()

    def arrive():
        own_side.wait()
        landed(fs.at[pl.ds(0, n // 2 - 1)], s_r.at[0])
        landed(us, u_r.at[0])

    reduce_phase(
        copies, f, fs, u, us, arrive, q, tot, keep,
        a_out, a_in, b_out, b_in, e_out, e_in, h_out, h_in, g_out, g_in, a_r, b_r, e_r,
    )
    with jax.named_scope("drain"):
        q_out = pltpu.make_async_copy(q, q_ref, out_sem.at[5])
        q_out.start()
        q_out.wait()
        for copy in outs:
            copy.wait()
        for at, units in enumerate((n - 1, n - 1, n // 2 + 3, n // 2 - 1)):
            landed(f.at[pl.ds(0, units)], send.at[at])


def fused_step(n, rate, inputs, out_grads, weights, left_stats, right_stats, left_roots, right_roots, refresh):
    rows, width = out_grads.shape
    block = weights.shape[1]
    nz = n // LINE
    dma = pltpu.SemaphoreType.DMA
    anywhere = pl.BlockSpec(memory_space=pl.ANY)
    square = pltpu.VMEM((block, block), F32)
    narrow = pltpu.VMEM((block, block), BF16)
    cut = rows // 4
    shards = pltpu.VMEM((nz, rows - cut, width), BF16)
    return pl.pallas_call(
        functools.partial(step_kernel, n, rate),
        out_shape=[jax.ShapeDtypeStruct((1, block, block), F32)] * 5 + [jax.ShapeDtypeStruct((rows, width), BF16)],
        in_specs=[pl.BlockSpec(memory_space=pltpu.SMEM)] + [pl.BlockSpec(memory_space=pltpu.HBM)] * 7,
        out_specs=[anywhere] * 6,
        scratch_shapes=[
            pltpu.VMEM((n, rows, block), BF16), pltpu.VMEM((n // 2, rows, block), BF16), pltpu.VMEM((n, rows, width), BF16),
        ] + [square] * 7 + [narrow] * 2 + [pltpu.VMEM((rows, width), BF16)] + [pltpu.VMEM((nz, rows, width), F32), pltpu.VMEM((2, cut, width), F32)] + [shards] * 4
        + [pltpu.VMEM((4, cut, width), BF16)] * 2 + [pltpu.VMEM((2, cut, width), BF16)] * 2 + [pltpu.VMEM((cut, width), BF16)] * 2
        + [dma((5,)), dma((6,)), dma((4,)), dma((3,))]
        + [dma((n + len(EXTRA) - 1,)), dma((n // 2,)), dma((LINE,)), dma((LINE,)), dma((2 * LINE,)), dma((1,)), dma((1,))]
        + [dma((2 * LINE,)), dma((2 * LINE,)), dma((5,))],
        compiler_params=pltpu.CompilerParams(collective_id=0, has_side_effects=True, vmem_limit_bytes=48 << 20),
        name="fused_step",
    )(refresh, inputs, pltpu.with_memory_space_constraint(out_grads, pltpu.HBM), weights, left_stats, right_stats, left_roots, right_roots)


def hand_out_kernel(*refs):
    count = len(refs) // 2
    copies = [pltpu.make_async_copy(refs[k], refs[count + k], refs[-1].at[k]) for k in range(count)]
    for copy in copies:
        copy.start()
    for copy in copies:
        copy.wait()


def hand_out(*arrays):
    anywhere = pl.BlockSpec(memory_space=pl.ANY)
    return pl.pallas_call(
        hand_out_kernel,
        out_shape=[jax.ShapeDtypeStruct(a.shape, a.dtype) for a in arrays],
        in_specs=[anywhere] * len(arrays),
        out_specs=[pl.BlockSpec(memory_space=pltpu.HBM)] * len(arrays),
        scratch_shapes=[pltpu.SemaphoreType.DMA((len(arrays),))],
        compiler_params=pltpu.CompilerParams(vmem_limit_bytes=1 << 20),
        name="hand_out",
    )(*arrays)


def body(inputs, out_grads, weights, left_stats, right_stats, left_roots, right_roots, refresh):
    tok_local, model_width = inputs.shape
    block = weights.shape[1]
    col_count = out_grads.shape[1]
    row_blocks = model_width // block
    col_blocks = col_count // block
    replicas = lax.axis_size("dp")
    tok_total = tok_local * replicas
    kernels = col_blocks == 1 and lax.axis_size("owner") == 2 and replicas == 4 * LINE and block == 4 * tok_local
    rate = 0.25 / math.sqrt(model_width)
    if kernels:
        return hand_out(*fused_step(
            replicas, rate, inputs, out_grads, weights, left_stats, right_stats, left_roots, right_roots, refresh
        ))
    mine = lax.axis_index("dp") % col_blocks
    grads = lax.all_gather(out_grads, "dp", axis=0, tiled=True)
    grads = lax.dynamic_slice_in_dim(grads, mine * block, block, 1)
    send = jnp.repeat(inputs.reshape(tok_local, row_blocks, block).transpose(1, 0, 2), col_blocks, axis=0)
    features = lax.all_to_all(send, "dp", split_axis=0, concat_axis=0, tiled=True)
    features = features.reshape(tok_total, block)
    gradient = dot(features, grads, ((0,), (0,))) / tok_total
    left_new = BETA * left_stats[0] + (1.0 - BETA) * dot(gradient, gradient, ((1,), (1,)))
    right_new = BETA * right_stats[0] + (1.0 - BETA) * dot(gradient, gradient, ((0,), (0,)))
    left_root, right_root = lax.cond(
        refresh[0] > 0, roots, stale, left_new, right_new, left_roots[0], right_roots[0]
    )
    direction = dot3(dot3(left_root, gradient), right_root)
    direction = direction * (block / jnp.sqrt(jnp.sum(direction * direction) + 1e-12))
    updated = (weights[0] - rate * direction).astype(BF16)
    partial = dot(features, updated).astype(BF16)
    if col_blocks > 1:
        partial = lax.dynamic_update_slice(jnp.zeros((tok_total, col_count), BF16), partial, (0, mine * block))
    queries = lax.psum_scatter(partial, "dp", scatter_dimension=0, tiled=True)
    return (left_new[None], right_new[None], left_root[None], right_root[None], direction[None], queries)


def solution(mesh):
    blocks = P(("dp", "owner"), None, None)
    in_specs = (P("dp", None), P("dp", "owner"), blocks, blocks, blocks, blocks, blocks, P(("dp", "owner")))
    out_specs = (blocks,) * 5 + (P("dp", "owner"),)
    return jax.shard_map(body, mesh=mesh, in_specs=in_specs, out_specs=out_specs, check_vma=False)
```

```python
import functools
import math

import jax
import jax.numpy as jnp
from jax import lax
from jax.experimental import pallas as pl
from jax.experimental.pallas import tpu as pltpu
from jax.sharding import PartitionSpec as P

BETA = 0.95
DAMPING = 0.0001
BF16 = jnp.bfloat16
F32 = jnp.float32


def dot(a, b, dims=((1,), (0,))):
    return lax.dot_general(a.astype(BF16), b.astype(BF16), (dims, ((), ())), preferred_element_type=F32)


def split(a):
    high = a.astype(BF16)
    return high, (a - high.astype(F32)).astype(BF16)


def dot3(a, b):
    a_high, a_low = split(a)
    b_high, b_low = split(b)
    return dot(a_high, b_high) + (dot(a_high, b_low) + dot(a_low, b_high))


def even_dot(a, b, dims=((1,), (0,))):
    half = a.shape[0] // 2
    a, b = a.astype(BF16), b.astype(BF16)

    def cut(x, axis, low):
        return (x[:half] if low else x[half:]) if axis == 0 else (x[:, :half] if low else x[:, half:])

    over, under = (cut(a, 1 - dims[0][0], low) for low in (True, False))
    upper = dot(over, b, dims)
    corner = dot(under, cut(b, 1 - dims[1][0], False), dims)
    return jnp.concatenate([upper, jnp.concatenate([upper[:, half:].T, corner], axis=1)], axis=0)


def inverse_roots(*statistics):
    shape = statistics[0].shape
    eye = (lax.broadcasted_iota(jnp.int32, shape, 0) == lax.broadcasted_iota(jnp.int32, shape, 1)).astype(F32)
    damped = [s + DAMPING * eye for s in statistics]
    squares = [even_dot(a, a) for a in damped]
    z = [2.5 / jnp.sqrt(jnp.sum(a * a, keepdims=True)) for a in damped]
    m = [scale * a for scale, a in zip(z, damped)]
    p = [(scale * scale) * a for scale, a in zip(z, squares)]
    q = [even_dot(b, a) for a, b in zip(m, p)]
    r = [1.5625 * a - 0.625 * b + 0.0625 * c for a, b, c in zip(m, p, q)]
    w = [0.0625 * c + 0.1953125 * a - 0.01953125 * b for a, b, c in zip(m, p, r)]
    last = [even_dot(a, b) for a, b in zip(w, r)]
    return tuple(
        jnp.sqrt(jnp.sqrt(scale)) * (1.5625 * eye - 0.3125 * a - 0.48828125 * b + c)
        for scale, a, b, c in zip(z, m, r, last)
    )


def roots(left_stat, right_stat, left_old, right_old):
    return inverse_roots(left_stat, right_stat)


def stale(left_stat, right_stat, left_old, right_old):
    return (left_old, right_old)

LINE = 4


def flip(index, stride):
    return index + stride - 2 * stride * lax.rem(lax.div(index, stride), 2)


def remote(src, dst, send, recv, peer):
    return pltpu.make_async_remote_copy(
        src_ref=src, dst_ref=dst, send_sem=send, recv_sem=recv,
        device_id=peer, device_id_type=pl.DeviceIdType.MESH,
    )


def greet(peers):
    barrier = pltpu.get_barrier_semaphore()
    for peer in peers:
        pl.semaphore_signal(barrier, inc=1, device_id=peer, device_id_type=pl.DeviceIdType.MESH)
    pl.semaphore_wait(barrier, len(peers))


def toggle(index, bits):
    stride = 1
    while stride <= bits:
        if bits & stride:
            index = flip(index, stride)
        stride *= 2
    return index


ORDER = (
    "g", "x1", "x10", "x2", "x14", "x3", "x4", "h", "x6", "x11", "x15", "x5", "x8", "x7", "x12", "x9",
    "x13", "i1", "p1", "p2", "p4", "p10", "y0", "p3", "i3", "p14", "p6", "p11", "y2", "p15", "d0", "p5",
    "p7", "y1", "d2", "p8", "p12", "d10", "p9", "p13", "y3", "d14", "s3", "s11", "s15", "d6", "s7", "d4",
    "s5", "d8", "s9", "d12", "s13",
)


PARTS = {9: 2, 13: 2}
EXTRA = {(9, 1): 0, (13, 1): 16}


def landed(view, sem):
    pltpu.make_async_copy(view, view, sem).wait()


HIGH = (
    "o3", "s3", "o1", "t3", "o2", "s2", "t1", "o0", "p30", "t2", "p31", "h", "s1", "s0", "t0",
    "p20", "p21", "g", "p10", "p11", "f", "q0", "q1",
)
LOW = (
    "o1", "s1", "o3", "s3", "t1", "o2", "t3", "o0", "p10", "t2", "p11", "h", "s2", "s0", "t0",
    "p30", "p31", "g", "p20", "p21", "f", "q0", "q1",
)


class Copies:
    def __init__(self, send):
        self.send = send

    def group(self, at):
        def go(src, dst, recv, peer):
            copy = remote(src, dst, self.send.at[at], recv, peer)
            copy.start()
            return copy

        return go


def gather_phase(n, copies, x_ref, g_ref, f, fs, ga, grad, own, x_r, p_r, z_r, y_r, c_r, s_r):
    me, mine = lax.axis_index("dp"), lax.axis_index("owner")
    rows, width = g_ref.shape
    half = rows // 2
    far = pl.ds(pl.multiple_of((1 - mine) * half, half), half)
    pair, row = flip(me, 1), flip(me, 2)
    go_x, go_g, go_s = copies.group(0), copies.group(1), copies.group(2)

    def cols(block):
        return pl.ds(pl.multiple_of(block * width, width), width)

    own_in = [
        pltpu.make_async_copy(x_ref.at[:, cols(me)], f.at[me], own.at[0]),
        pltpu.make_async_copy(g_ref, ga.at[me], own.at[1]),
        pltpu.make_async_copy(x_ref.at[:, cols(pair)], fs.at[lax.div(me, 2)], own.at[2]),
    ]
    x_copy, z_copy, y_copy, c_copy = {}, {}, {}, {}

    def fan(t, block):
        slot = toggle(me, LINE * t)
        y_copy[t] = go_g(block, ga.at[slot], y_r.at[t], (row, mine))
        c_copy[t] = go_g(block, ga.at[slot], c_r.at[t], (pair, mine))

    def g(_):
        for copy in own_in:
            copy.start()
        for t in (2, 1):
            z_copy[t] = go_g(g_ref, ga.at[me], z_r.at[t], (toggle(me, LINE * t), mine))
        fan(0, g_ref)

    def h(_):
        z_copy[2].wait_recv()
        held = ga.at[toggle(me, LINE * 2)]
        z_copy[3] = go_g(held, held, z_r.at[3], (toggle(me, LINE), mine))
        fan(2, held)

    def i(t):
        z_copy[t].wait_recv()
        fan(t, ga.at[toggle(me, LINE * t)])

    def y(t):
        y_copy[t].wait_recv()
        held = ga.at[toggle(row, LINE * t)]
        c_copy[LINE + t] = go_g(held, held, c_r.at[LINE + t], (pair, mine))

    def slices(k):
        count = PARTS.get(k, 1)
        span = half // count
        return [pl.ds(pl.multiple_of(mine * half + at * span, span), span) for at in range(count)]

    def x(k):
        peer = toggle(me, k)
        if k == 1:
            x_copy[k] = [go_x(x_ref.at[:, cols(peer)], f.at[me], x_r.at[k], (peer, mine))]
            return
        x_copy[k] = []
        for at, part in enumerate(slices(k)):
            sem = x_r.at[k if at == 0 else EXTRA[k, at]]
            x_copy[k].append(go_x(x_ref.at[part, cols(peer)], f.at[me, part], sem, (peer, mine)))

    def p(k):
        if k == 1:
            x_copy[k][0].wait_recv()
            return
        for at, part in enumerate(slices(k)):
            x_copy[k][at].wait_recv()
            held = f.at[toggle(me, k), part]
            go_x(held, held, p_r.at[k // 2], (me, 1 - mine))

    def d(k):
        chip = pl.ds(pl.multiple_of(2 * lax.div(toggle(me, k), 2), 2), 2)
        if k:
            landed(f.at[chip, far], p_r.at[k // 2])
        else:
            own_in[0].wait()
            own_in[1].wait()
        t = k // LINE
        c_copy[t + LINE if k % LINE else t].wait_recv()
        term = dot(f[chip].reshape(2 * rows, width), ga[chip].reshape(2 * rows, width), ((0,), (0,)))
        grad[...] = term if k == 0 else grad[...] + term

    def s(k):
        source = toggle(me, k)
        go_s(f.at[source], fs.at[lax.div(source, 2)], s_r.at[0], (pair, mine))

    steps = dict(g=g, h=h, i=i, y=y, x=x, p=p, d=d, s=s)
    for word in ORDER:
        with jax.named_scope(word):
            steps[word[0]](int(word[1:] or 0))
    return own_in[2]


def reduce_phase(order, copies, feats, fs, u, us, arrive, q, tot, keep, a_out, a_in, b_out, b_in, e_out, e_in, h_out, h_in, g_out, g_in,
                 a_r, b_r, e_r):
    me, mine = lax.axis_index("dp"), lax.axis_index("owner")
    row = flip(me, 2)
    rows = q.shape[0]
    cut = rows // 4
    half = (rows - cut) // 2
    go = copies.group(3)
    first = pl.ds(0, cut)
    rest = [pl.ds(cut + k * half, half) for k in range(2)]
    spans = [pl.ds(k * half, half) for k in range(2)]
    near_z, far_z, direct, across = (toggle(me, LINE), mine), (toggle(me, 2 * LINE), mine), (toggle(me, 3 * LINE), mine), (row, mine)

    def near_part(base, t):
        return dot(feats[toggle(base, LINE * t)], u[...])

    def far_part(base, t):
        return dot(fs[lax.div(toggle(base, LINE * t), 2)], us[...])

    a_copy, b_copy, h_copy, g_copy = {}, {}, [], []
    lead = int(order[0][1])
    ahead = near_part(row, lead)
    with jax.named_scope("swap"):
        arrive()

    def o(t):
        value = (ahead if t == lead else near_part(row, t)) + far_part(row, t)
        a_out[t] = value[cut:].astype(BF16)
        if t % 2:
            early(0 if t == 3 else 1, value)
        else:
            keep[0 if t == 2 else 1] = value[:cut]

    def t(t):
        value = near_part(me, t) + far_part(me, t)
        if t % 2:
            early(2 if t == 3 else 3, value)
        tot[t] = value

    def early(k, value):
        e_out[k] = value[:cut].astype(BF16)
        go(e_out.at[k], e_in.at[k], e_r.at[k // 2], near_z)

    def s(t):
        for k in range(2):
            a_copy[t, k] = go(a_out.at[t, spans[k]], a_in.at[t, spans[k]], a_r.at[2 * t + k], across)

    def p(t, k):
        a_copy[t, k].wait_recv()
        value = tot[t, rest[k]] + a_in[t, spans[k]].astype(F32)
        peer = near_z
        if t == 2:
            peer = far_z
            if k:
                b_copy[3, k].wait_recv()
                value = value + b_in[3, spans[k]].astype(F32)
        elif (t, k) == (3, 0):
            peer = direct
        b_out[t, spans[k]] = value.astype(BF16)
        b_copy[t, k] = go(b_out.at[t, spans[k]], b_in.at[t, spans[k]], b_r.at[2 * t + k], peer)

    def h():
        landed(e_in.at[pl.ds(0, 2)], e_r.at[0])
        for k in range(2):
            h_out[k] = (keep[k] + e_in[k].astype(F32)).astype(BF16)
            h_copy.append(go(h_out.at[k], h_in.at[k], e_r.at[3 + k], across))

    def g():
        landed(e_in.at[pl.ds(2, 2)], e_r.at[1])
        h_copy[0].wait_recv()
        g_out[...] = (tot[2, first] + e_in[2].astype(F32) + h_in[0].astype(F32)).astype(BF16)
        g_copy.append(go(g_out, g_in, e_r.at[2], far_z))

    def f():
        h_copy[1].wait_recv()
        g_copy[0].wait_recv()
        q[first] = (tot[0, first] + e_in[3].astype(F32) + h_in[1].astype(F32) + g_in[...].astype(F32)).astype(BF16)

    def q_(k):
        a_copy[0, k].wait_recv()
        value = tot[0, rest[k]] + a_in[0, spans[k]].astype(F32)
        for at in (2, 1) if k else (3, 2, 1):
            b_copy[at, k].wait_recv()
            value = value + b_in[at, spans[k]].astype(F32)
        q[rest[k]] = value.astype(BF16)

    steps = dict(o=o, t=t, s=s, p=p, h=h, g=g, f=f, q=q_)
    for word in order:
        with jax.named_scope("r" + word):
            steps[word[0]](*map(int, word[1:]))


def step_kernel(n, rate, flag, x_ref, g_ref, w_hbm, ls_hbm, rs_hbm, lr_hbm, rr_hbm,
                ls_out, rs_out, lr_out, rr_out, d_out, q_ref,
                f, fs, ga, grad, w, ls, rs, lr, rr, d, u, us, q, tot, keep, a_out, a_in, b_out, b_in, e_out, e_in, h_out, h_in, g_out, g_in,
                in_sem, out_sem, send, own, x_r, p_r, z_r, y_r, c_r, s_r, u_r, a_r, b_r, e_r):
    me, mine = lax.axis_index("dp"), lax.axis_index("owner")
    pair = flip(me, 1)
    block = w.shape[0]
    with jax.named_scope("greet"):
        greet([(toggle(me, k), mine) for k in range(1, n)] + [(me, 1 - mine)])
    copies = Copies(send)
    ins = [
        pltpu.make_async_copy(src.at[0], dst, in_sem.at[k])
        for k, (src, dst) in enumerate(((ls_hbm, ls), (rs_hbm, rs), (lr_hbm, lr), (rr_hbm, rr), (w_hbm, w)))
    ]
    for copy in ins:
        copy.start()
    own_side = gather_phase(n, copies, x_ref, g_ref, f, fs, ga, grad, own, x_r, p_r, z_r, y_r, c_r, s_r)
    outs = [
        pltpu.make_async_copy(src, dst.at[0], out_sem.at[k])
        for k, (src, dst) in enumerate(((ls, ls_out), (rs, rs_out), (lr, lr_out), (rr, rr_out), (d, d_out)))
    ]
    with jax.named_scope("stats"):
        for copy in ins:
            copy.wait()
        high = (grad[...] * (1.0 / (n * g_ref.shape[0]))).astype(BF16)
        ls[...] = BETA * ls[...] + (1.0 - BETA) * even_dot(high, high, ((1,), (1,)))
        rs[...] = BETA * rs[...] + (1.0 - BETA) * even_dot(high, high, ((0,), (0,)))
        outs[0].start()
        outs[1].start()
    with jax.named_scope("roots"):
        anew = jnp.full((block, block), flag[0], jnp.int32) > 0
        left, right = inverse_roots(ls[...], rs[...])
        lr[...] = jnp.where(anew, left, lr[...])
        rr[...] = jnp.where(anew, right, rr[...])
        outs[2].start()
        outs[3].start()
    with jax.named_scope("direction"):
        through = dot(lr[...], high).astype(BF16)
        last = rr[...].astype(BF16)
        total = jnp.zeros((8, block), F32)
        for k in range(4):
            span = block // 4
            value = dot(through[k * span : (k + 1) * span], last)
            d[pl.ds(k * span, span)] = value
            total = total + jnp.sum((value * value).reshape(span // 8, 8, block), axis=0)
    with jax.named_scope("update"):
        scale = block / jnp.sqrt(jnp.sum(total, keepdims=True) + 1e-12)
    for k in range(2):
        with jax.named_scope(f"weights{k}"):
            part = pl.ds(k * block // 2, block // 2)
            u[part] = (w[part] - (rate * scale) * d[part]).astype(BF16)
            copies.group(2)(u.at[part], us.at[part], u_r.at[0], (pair, mine))
    with jax.named_scope("scaled"):
        d[...] = scale * d[...]
        outs[4].start()

    def arrive():
        own_side.wait()
        landed(fs.at[pl.ds(0, n // 2 - 1)], s_r.at[0])
        landed(us, u_r.at[0])

    def reduce_in(order):
        reduce_phase(
            order, copies, f, fs, u, us, arrive, q, tot, keep,
            a_out, a_in, b_out, b_in, e_out, e_in, h_out, h_in, g_out, g_in, a_r, b_r, e_r,
        )

    low = lax.div(me, LINE) < LINE // 2
    pl.when(low)(functools.partial(reduce_in, LOW))
    pl.when(jnp.logical_not(low))(functools.partial(reduce_in, HIGH))
    with jax.named_scope("drain"):
        q_out = pltpu.make_async_copy(q, q_ref, out_sem.at[5])
        q_out.start()
        q_out.wait()
        for copy in outs:
            copy.wait()
        for at, units in enumerate((n - 1, n - 1, n // 2 + 3, n // 2 - 1)):
            landed(f.at[pl.ds(0, units)], send.at[at])


def fused_step(n, rate, inputs, out_grads, weights, left_stats, right_stats, left_roots, right_roots, refresh):
    rows, width = out_grads.shape
    block = weights.shape[1]
    nz = n // LINE
    dma = pltpu.SemaphoreType.DMA
    anywhere = pl.BlockSpec(memory_space=pl.ANY)
    square = pltpu.VMEM((block, block), F32)
    narrow = pltpu.VMEM((block, block), BF16)
    cut = rows // 4
    shards = pltpu.VMEM((nz, rows - cut, width), BF16)
    return pl.pallas_call(
        functools.partial(step_kernel, n, rate),
        out_shape=[jax.ShapeDtypeStruct((1, block, block), F32)] * 5 + [jax.ShapeDtypeStruct((rows, width), BF16)],
        in_specs=[pl.BlockSpec(memory_space=pltpu.SMEM)] + [pl.BlockSpec(memory_space=pltpu.HBM)] * 7,
        out_specs=[anywhere] * 6,
        scratch_shapes=[
            pltpu.VMEM((n, rows, block), BF16), pltpu.VMEM((n // 2, rows, block), BF16), pltpu.VMEM((n, rows, width), BF16),
        ] + [square] * 7 + [narrow] * 2 + [pltpu.VMEM((rows, width), BF16)] + [pltpu.VMEM((nz, rows, width), F32), pltpu.VMEM((2, cut, width), F32)] + [shards] * 4
        + [pltpu.VMEM((4, cut, width), BF16)] * 2 + [pltpu.VMEM((2, cut, width), BF16)] * 2 + [pltpu.VMEM((cut, width), BF16)] * 2
        + [dma((5,)), dma((6,)), dma((4,)), dma((3,))]
        + [dma((n + len(EXTRA) - 1,)), dma((n // 2,)), dma((LINE,)), dma((LINE,)), dma((2 * LINE,)), dma((1,)), dma((1,))]
        + [dma((2 * LINE,)), dma((2 * LINE,)), dma((5,))],
        compiler_params=pltpu.CompilerParams(collective_id=0, has_side_effects=True, vmem_limit_bytes=48 << 20),
        name="fused_step",
    )(refresh, inputs, pltpu.with_memory_space_constraint(out_grads, pltpu.HBM), weights, left_stats, right_stats, left_roots, right_roots)


def hand_out_kernel(*refs):
    count = len(refs) // 2
    copies = [pltpu.make_async_copy(refs[k], refs[count + k], refs[-1].at[k]) for k in range(count)]
    for copy in copies:
        copy.start()
    for copy in copies:
        copy.wait()


def hand_out(*arrays):
    anywhere = pl.BlockSpec(memory_space=pl.ANY)
    return pl.pallas_call(
        hand_out_kernel,
        out_shape=[jax.ShapeDtypeStruct(a.shape, a.dtype) for a in arrays],
        in_specs=[anywhere] * len(arrays),
        out_specs=[pl.BlockSpec(memory_space=pltpu.HBM)] * len(arrays),
        scratch_shapes=[pltpu.SemaphoreType.DMA((len(arrays),))],
        compiler_params=pltpu.CompilerParams(vmem_limit_bytes=1 << 20),
        name="hand_out",
    )(*arrays)


def body(inputs, out_grads, weights, left_stats, right_stats, left_roots, right_roots, refresh):
    tok_local, model_width = inputs.shape
    block = weights.shape[1]
    col_count = out_grads.shape[1]
    row_blocks = model_width // block
    col_blocks = col_count // block
    replicas = lax.axis_size("dp")
    tok_total = tok_local * replicas
    kernels = col_blocks == 1 and lax.axis_size("owner") == 2 and replicas == 4 * LINE and block == 4 * tok_local
    rate = 0.25 / math.sqrt(model_width)
    if kernels:
        return hand_out(*fused_step(
            replicas, rate, inputs, out_grads, weights, left_stats, right_stats, left_roots, right_roots, refresh
        ))
    mine = lax.axis_index("dp") % col_blocks
    grads = lax.all_gather(out_grads, "dp", axis=0, tiled=True)
    grads = lax.dynamic_slice_in_dim(grads, mine * block, block, 1)
    send = jnp.repeat(inputs.reshape(tok_local, row_blocks, block).transpose(1, 0, 2), col_blocks, axis=0)
    features = lax.all_to_all(send, "dp", split_axis=0, concat_axis=0, tiled=True)
    features = features.reshape(tok_total, block)
    gradient = dot(features, grads, ((0,), (0,))) / tok_total
    left_new = BETA * left_stats[0] + (1.0 - BETA) * dot(gradient, gradient, ((1,), (1,)))
    right_new = BETA * right_stats[0] + (1.0 - BETA) * dot(gradient, gradient, ((0,), (0,)))
    left_root, right_root = lax.cond(
        refresh[0] > 0, roots, stale, left_new, right_new, left_roots[0], right_roots[0]
    )
    direction = dot3(dot3(left_root, gradient), right_root)
    direction = direction * (block / jnp.sqrt(jnp.sum(direction * direction) + 1e-12))
    updated = (weights[0] - rate * direction).astype(BF16)
    partial = dot(features, updated).astype(BF16)
    if col_blocks > 1:
        partial = lax.dynamic_update_slice(jnp.zeros((tok_total, col_count), BF16), partial, (0, mine * block))
    queries = lax.psum_scatter(partial, "dp", scatter_dimension=0, tiled=True)
    return (left_new[None], right_new[None], left_root[None], right_root[None], direction[None], queries)


def solution(mesh):
    blocks = P(("dp", "owner"), None, None)
    in_specs = (P("dp", None), P("dp", "owner"), blocks, blocks, blocks, blocks, blocks, P(("dp", "owner")))
    out_specs = (blocks,) * 5 + (P("dp", "owner"),)
    return jax.shard_map(body, mesh=mesh, in_specs=in_specs, out_specs=out_specs, check_vma=False)
```

```python
import functools
import math

import jax
import jax.numpy as jnp
from jax import lax
from jax.experimental import pallas as pl
from jax.experimental.pallas import tpu as pltpu
from jax.sharding import PartitionSpec as P

BETA = 0.95
DAMPING = 0.0001
BF16 = jnp.bfloat16
F32 = jnp.float32


def dot(a, b, dims=((1,), (0,))):
    return lax.dot_general(a.astype(BF16), b.astype(BF16), (dims, ((), ())), preferred_element_type=F32)


def split(a):
    high = a.astype(BF16)
    return high, (a - high.astype(F32)).astype(BF16)


def dot3(a, b):
    a_high, a_low = split(a)
    b_high, b_low = split(b)
    return dot(a_high, b_high) + (dot(a_high, b_low) + dot(a_low, b_high))


def even_dot(a, b, dims=((1,), (0,))):
    half = a.shape[0] // 2
    a, b = a.astype(BF16), b.astype(BF16)

    def cut(x, axis, low):
        return (x[:half] if low else x[half:]) if axis == 0 else (x[:, :half] if low else x[:, half:])

    over, under = (cut(a, 1 - dims[0][0], low) for low in (True, False))
    upper = dot(over, b, dims)
    corner = dot(under, cut(b, 1 - dims[1][0], False), dims)
    return jnp.concatenate([upper, jnp.concatenate([upper[:, half:].T, corner], axis=1)], axis=0)


def inverse_roots(*statistics):
    shape = statistics[0].shape
    eye = (lax.broadcasted_iota(jnp.int32, shape, 0) == lax.broadcasted_iota(jnp.int32, shape, 1)).astype(F32)
    damped = [s + DAMPING * eye for s in statistics]
    squares = [even_dot(a, a) for a in damped]
    z = [2.5 / jnp.sqrt(jnp.sum(a * a, keepdims=True)) for a in damped]
    m = [scale * a for scale, a in zip(z, damped)]
    p = [(scale * scale) * a for scale, a in zip(z, squares)]
    q = [even_dot(b, a) for a, b in zip(m, p)]
    r = [1.5625 * a - 0.625 * b + 0.0625 * c for a, b, c in zip(m, p, q)]
    w = [0.0625 * c + 0.1953125 * a - 0.01953125 * b for a, b, c in zip(m, p, r)]
    last = [even_dot(a, b) for a, b in zip(w, r)]
    return tuple(
        jnp.sqrt(jnp.sqrt(scale)) * (1.5625 * eye - 0.3125 * a - 0.48828125 * b + c)
        for scale, a, b, c in zip(z, m, r, last)
    )


def roots(left_stat, right_stat, left_old, right_old):
    return inverse_roots(left_stat, right_stat)


def stale(left_stat, right_stat, left_old, right_old):
    return (left_old, right_old)

LINE = 4


def flip(index, stride):
    return index + stride - 2 * stride * lax.rem(lax.div(index, stride), 2)


def remote(src, dst, send, recv, peer):
    return pltpu.make_async_remote_copy(
        src_ref=src, dst_ref=dst, send_sem=send, recv_sem=recv,
        device_id=peer, device_id_type=pl.DeviceIdType.MESH,
    )


def greet(peers):
    barrier = pltpu.get_barrier_semaphore()
    for peer in peers:
        pl.semaphore_signal(barrier, inc=1, device_id=peer, device_id_type=pl.DeviceIdType.MESH)
    pl.semaphore_wait(barrier, len(peers))


def toggle(index, bits):
    stride = 1
    while stride <= bits:
        if bits & stride:
            index = flip(index, stride)
        stride *= 2
    return index


ORDER = (
    "g", "x1", "x10", "x2", "x14", "x3", "x4", "h", "x6", "x11", "x15", "x5", "x8", "x7", "x12", "x9",
    "x13", "i1", "p1", "p2", "p4", "p10", "y0", "p3", "i3", "p14", "p6", "p11", "y2", "p15", "d0", "p5",
    "p7", "y1", "d2", "p8", "p12", "d10", "p9", "p13", "y3", "d14", "s3", "s11", "s15", "d6", "s7", "d4",
    "s5", "d8", "s9", "d12", "s13",
)


PARTS = {9: 2, 13: 2}
EXTRA = {(9, 1): 0, (13, 1): 16}


def landed(view, sem):
    pltpu.make_async_copy(view, view, sem).wait()


SPANS = 3
DIRECT = (0,)
HIGH = (
    "o3", "s3", "o1", "t3", "o2", "s2", "t1", "o0", "p30", "t2", "p31", "p32", "h", "s1", "s0", "t0",
    "p20", "p21", "p22", "g", "p10", "p11", "p12", "f", "q0", "q1", "q2",
)
LOW = (
    "o1", "s1", "o3", "s3", "t1", "o2", "t3", "o0", "p10", "t2", "p11", "p12", "s2", "h", "s0", "t0",
    "p30", "p31", "p32", "p20", "p21", "p22", "g", "f", "q0", "q1", "q2",
)


class Copies:
    def __init__(self, send):
        self.send = send

    def group(self, at):
        def go(src, dst, recv, peer):
            copy = remote(src, dst, self.send.at[at], recv, peer)
            copy.start()
            return copy

        return go


def gather_phase(n, copies, x_ref, g_ref, f, fs, ga, grad, own, x_r, p_r, z_r, y_r, c_r, s_r):
    me, mine = lax.axis_index("dp"), lax.axis_index("owner")
    rows, width = g_ref.shape
    half = rows // 2
    far = pl.ds(pl.multiple_of((1 - mine) * half, half), half)
    pair, row = flip(me, 1), flip(me, 2)
    go_x, go_g, go_s = copies.group(0), copies.group(1), copies.group(2)

    def cols(block):
        return pl.ds(pl.multiple_of(block * width, width), width)

    own_in = [
        pltpu.make_async_copy(x_ref.at[:, cols(me)], f.at[me], own.at[0]),
        pltpu.make_async_copy(g_ref, ga.at[me], own.at[1]),
        pltpu.make_async_copy(x_ref.at[:, cols(pair)], fs.at[lax.div(me, 2)], own.at[2]),
    ]
    x_copy, z_copy, y_copy, c_copy = {}, {}, {}, {}

    def fan(t, block):
        slot = toggle(me, LINE * t)
        y_copy[t] = go_g(block, ga.at[slot], y_r.at[t], (row, mine))
        c_copy[t] = go_g(block, ga.at[slot], c_r.at[t], (pair, mine))

    def g(_):
        for copy in own_in:
            copy.start()
        for t in (2, 1):
            z_copy[t] = go_g(g_ref, ga.at[me], z_r.at[t], (toggle(me, LINE * t), mine))
        fan(0, g_ref)

    def h(_):
        z_copy[2].wait_recv()
        held = ga.at[toggle(me, LINE * 2)]
        z_copy[3] = go_g(held, held, z_r.at[3], (toggle(me, LINE), mine))
        fan(2, held)

    def i(t):
        z_copy[t].wait_recv()
        fan(t, ga.at[toggle(me, LINE * t)])

    def y(t):
        y_copy[t].wait_recv()
        held = ga.at[toggle(row, LINE * t)]
        c_copy[LINE + t] = go_g(held, held, c_r.at[LINE + t], (pair, mine))

    def slices(k):
        count = PARTS.get(k, 1)
        span = half // count
        return [pl.ds(pl.multiple_of(mine * half + at * span, span), span) for at in range(count)]

    def x(k):
        peer = toggle(me, k)
        if k == 1:
            x_copy[k] = [go_x(x_ref.at[:, cols(peer)], f.at[me], x_r.at[k], (peer, mine))]
            return
        x_copy[k] = []
        for at, part in enumerate(slices(k)):
            sem = x_r.at[k if at == 0 else EXTRA[k, at]]
            x_copy[k].append(go_x(x_ref.at[part, cols(peer)], f.at[me, part], sem, (peer, mine)))

    def p(k):
        if k == 1:
            x_copy[k][0].wait_recv()
            return
        for at, part in enumerate(slices(k)):
            x_copy[k][at].wait_recv()
            held = f.at[toggle(me, k), part]
            go_x(held, held, p_r.at[k // 2], (me, 1 - mine))

    def d(k):
        chip = pl.ds(pl.multiple_of(2 * lax.div(toggle(me, k), 2), 2), 2)
        if k:
            landed(f.at[chip, far], p_r.at[k // 2])
        else:
            own_in[0].wait()
            own_in[1].wait()
        t = k // LINE
        c_copy[t + LINE if k % LINE else t].wait_recv()
        term = dot(f[chip].reshape(2 * rows, width), ga[chip].reshape(2 * rows, width), ((0,), (0,)))
        grad[...] = term if k == 0 else grad[...] + term

    def s(k):
        source = toggle(me, k)
        go_s(f.at[source], fs.at[lax.div(source, 2)], s_r.at[0], (pair, mine))

    steps = dict(g=g, h=h, i=i, y=y, x=x, p=p, d=d, s=s)
    for word in ORDER:
        with jax.named_scope(word):
            steps[word[0]](int(word[1:] or 0))
    return own_in[2]


def reduce_phase(order, copies, feats, fs, u, us, arrive, q, tot, ahead, keep, a_out, a_in, b_out, b_in, e_out, e_in, h_out, h_in, g_out, g_in,
                 a_r, b_r, e_r):
    me, mine = lax.axis_index("dp"), lax.axis_index("owner")
    row = flip(me, 2)
    rows = q.shape[0]
    cut = rows // 4
    third = (rows - cut) // SPANS
    go = copies.group(3)
    first = pl.ds(0, cut)
    rest = [pl.ds(cut + k * third, third) for k in range(SPANS)]
    spans = [pl.ds(k * third, third) for k in range(SPANS)]
    near_z, far_z, direct, across = (toggle(me, LINE), mine), (toggle(me, 2 * LINE), mine), (toggle(me, 3 * LINE), mine), (row, mine)

    def near_part(base, t):
        return dot(feats[toggle(base, LINE * t)], u[...])

    def far_part(base, t):
        return dot(fs[lax.div(toggle(base, LINE * t), 2)], us[...])

    a_copy, b_copy, h_copy, g_copy = {}, {}, [], []
    for t in range(LINE):
        ahead[t] = near_part(row, t)
    with jax.named_scope("swap"):
        arrive()

    def o(t):
        value = ahead[t] + far_part(row, t)
        a_out[t] = value[cut:].astype(BF16)
        if t % 2:
            early(0 if t == 3 else 1, value)
        else:
            keep[0 if t == 2 else 1] = value[:cut]

    def t(t):
        value = near_part(me, t) + far_part(me, t)
        if t % 2:
            early(2 if t == 3 else 3, value)
        tot[t] = value

    def early(k, value):
        e_out[k] = value[:cut].astype(BF16)
        go(e_out.at[k], e_in.at[k], e_r.at[k // 2], near_z)

    def s(t):
        for k in range(SPANS):
            a_copy[t, k] = go(a_out.at[t, spans[k]], a_in.at[t, spans[k]], a_r.at[SPANS * t + k], across)

    def p(t, k):
        a_copy[t, k].wait_recv()
        value = tot[t, rest[k]] + a_in[t, spans[k]].astype(F32)
        peer = near_z
        if t == 2:
            peer = far_z
            if k not in DIRECT:
                b_copy[3, k].wait_recv()
                value = value + b_in[3, spans[k]].astype(F32)
        elif t == 3 and k in DIRECT:
            peer = direct
        b_out[t, spans[k]] = value.astype(BF16)
        b_copy[t, k] = go(b_out.at[t, spans[k]], b_in.at[t, spans[k]], b_r.at[SPANS * t + k], peer)

    def h():
        landed(e_in.at[pl.ds(0, 2)], e_r.at[0])
        for k in range(2):
            h_out[k] = (keep[k] + e_in[k].astype(F32)).astype(BF16)
            h_copy.append(go(h_out.at[k], h_in.at[k], e_r.at[3 + k], across))

    def g():
        landed(e_in.at[pl.ds(2, 2)], e_r.at[1])
        h_copy[0].wait_recv()
        g_out[...] = (tot[2, first] + e_in[2].astype(F32) + h_in[0].astype(F32)).astype(BF16)
        g_copy.append(go(g_out, g_in, e_r.at[2], far_z))

    def f():
        h_copy[1].wait_recv()
        g_copy[0].wait_recv()
        q[first] = (tot[0, first] + e_in[3].astype(F32) + h_in[1].astype(F32) + g_in[...].astype(F32)).astype(BF16)

    def q_(k):
        a_copy[0, k].wait_recv()
        value = tot[0, rest[k]] + a_in[0, spans[k]].astype(F32)
        for at in (3, 2, 1) if k in DIRECT else (2, 1):
            b_copy[at, k].wait_recv()
            value = value + b_in[at, spans[k]].astype(F32)
        q[rest[k]] = value.astype(BF16)

    steps = dict(o=o, t=t, s=s, p=p, h=h, g=g, f=f, q=q_)
    for word in order:
        with jax.named_scope("r" + word):
            steps[word[0]](*map(int, word[1:]))


def step_kernel(n, rate, flag, x_ref, g_ref, w_hbm, ls_hbm, rs_hbm, lr_hbm, rr_hbm,
                ls_out, rs_out, lr_out, rr_out, d_out, q_ref,
                f, fs, ga, grad, w, ls, rs, lr, rr, d, u, us, q, tot, ahead, keep, a_out, a_in, b_out, b_in, e_out, e_in, h_out, h_in, g_out, g_in,
                in_sem, out_sem, send, own, x_r, p_r, z_r, y_r, c_r, s_r, u_r, a_r, b_r, e_r):
    me, mine = lax.axis_index("dp"), lax.axis_index("owner")
    pair = flip(me, 1)
    block = w.shape[0]
    with jax.named_scope("greet"):
        greet([(toggle(me, k), mine) for k in range(1, n)] + [(me, 1 - mine)])
    copies = Copies(send)
    ins = [
        pltpu.make_async_copy(src.at[0], dst, in_sem.at[k])
        for k, (src, dst) in enumerate(((ls_hbm, ls), (rs_hbm, rs), (lr_hbm, lr), (rr_hbm, rr), (w_hbm, w)))
    ]
    for copy in ins:
        copy.start()
    own_side = gather_phase(n, copies, x_ref, g_ref, f, fs, ga, grad, own, x_r, p_r, z_r, y_r, c_r, s_r)
    outs = [
        pltpu.make_async_copy(src, dst.at[0], out_sem.at[k])
        for k, (src, dst) in enumerate(((ls, ls_out), (rs, rs_out), (lr, lr_out), (rr, rr_out), (d, d_out)))
    ]
    with jax.named_scope("stats"):
        for copy in ins:
            copy.wait()
        high = (grad[...] * (1.0 / (n * g_ref.shape[0]))).astype(BF16)
        ls[...] = BETA * ls[...] + (1.0 - BETA) * even_dot(high, high, ((1,), (1,)))
        rs[...] = BETA * rs[...] + (1.0 - BETA) * even_dot(high, high, ((0,), (0,)))
        outs[0].start()
        outs[1].start()
    with jax.named_scope("roots"):
        anew = jnp.full((block, block), flag[0], jnp.int32) > 0
        left, right = inverse_roots(ls[...], rs[...])
        lr[...] = jnp.where(anew, left, lr[...])
        rr[...] = jnp.where(anew, right, rr[...])
        outs[2].start()
        outs[3].start()
    with jax.named_scope("direction"):
        through = dot(lr[...], high).astype(BF16)
        last = rr[...].astype(BF16)
        total = jnp.zeros((8, block), F32)
        for k in range(4):
            span = block // 4
            value = dot(through[k * span : (k + 1) * span], last)
            d[pl.ds(k * span, span)] = value
            total = total + jnp.sum((value * value).reshape(span // 8, 8, block), axis=0)
    with jax.named_scope("update"):
        scale = block / jnp.sqrt(jnp.sum(total, keepdims=True) + 1e-12)
    for k in range(2):
        with jax.named_scope(f"weights{k}"):
            part = pl.ds(k * block // 2, block // 2)
            u[part] = (w[part] - (rate * scale) * d[part]).astype(BF16)
            copies.group(2)(u.at[part], us.at[part], u_r.at[0], (pair, mine))
    with jax.named_scope("scaled"):
        d[...] = scale * d[...]
        outs[4].start()

    def arrive():
        own_side.wait()
        landed(fs.at[pl.ds(0, n // 2 - 1)], s_r.at[0])
        landed(us, u_r.at[0])

    def reduce_in(order):
        reduce_phase(
            order, copies, f, fs, u, us, arrive, q, tot, ahead, keep,
            a_out, a_in, b_out, b_in, e_out, e_in, h_out, h_in, g_out, g_in, a_r, b_r, e_r,
        )

    low = lax.div(me, LINE) < LINE // 2
    pl.when(low)(functools.partial(reduce_in, LOW))
    pl.when(jnp.logical_not(low))(functools.partial(reduce_in, HIGH))
    with jax.named_scope("drain"):
        q_out = pltpu.make_async_copy(q, q_ref, out_sem.at[5])
        q_out.start()
        q_out.wait()
        for copy in outs:
            copy.wait()
        for at, units in enumerate((n - 1, n - 1, n // 2 + 3, n // 2 - 1)):
            landed(f.at[pl.ds(0, units)], send.at[at])


def fused_step(n, rate, inputs, out_grads, weights, left_stats, right_stats, left_roots, right_roots, refresh):
    rows, width = out_grads.shape
    block = weights.shape[1]
    nz = n // LINE
    dma = pltpu.SemaphoreType.DMA
    anywhere = pl.BlockSpec(memory_space=pl.ANY)
    square = pltpu.VMEM((block, block), F32)
    narrow = pltpu.VMEM((block, block), BF16)
    cut = rows // 4
    shards = pltpu.VMEM((nz, rows - cut, width), BF16)
    return pl.pallas_call(
        functools.partial(step_kernel, n, rate),
        out_shape=[jax.ShapeDtypeStruct((1, block, block), F32)] * 5 + [jax.ShapeDtypeStruct((rows, width), BF16)],
        in_specs=[pl.BlockSpec(memory_space=pltpu.SMEM)] + [pl.BlockSpec(memory_space=pltpu.HBM)] * 7,
        out_specs=[anywhere] * 6,
        scratch_shapes=[
            pltpu.VMEM((n, rows, block), BF16), pltpu.VMEM((n // 2, rows, block), BF16), pltpu.VMEM((n, rows, width), BF16),
        ] + [square] * 7 + [narrow] * 2 + [pltpu.VMEM((rows, width), BF16)] + [pltpu.VMEM((nz, rows, width), F32)] * 2 + [pltpu.VMEM((2, cut, width), F32)] + [shards] * 4
        + [pltpu.VMEM((4, cut, width), BF16)] * 2 + [pltpu.VMEM((2, cut, width), BF16)] * 2 + [pltpu.VMEM((cut, width), BF16)] * 2
        + [dma((5,)), dma((6,)), dma((4,)), dma((3,))]
        + [dma((n + len(EXTRA) - 1,)), dma((n // 2,)), dma((LINE,)), dma((LINE,)), dma((2 * LINE,)), dma((1,)), dma((1,))]
        + [dma((SPANS * LINE,)), dma((SPANS * LINE,)), dma((5,))],
        compiler_params=pltpu.CompilerParams(collective_id=0, has_side_effects=True, vmem_limit_bytes=48 << 20),
        name="fused_step",
    )(refresh, inputs, pltpu.with_memory_space_constraint(out_grads, pltpu.HBM), weights, left_stats, right_stats, left_roots, right_roots)


def hand_out_kernel(*refs):
    count = len(refs) // 2
    copies = [pltpu.make_async_copy(refs[k], refs[count + k], refs[-1].at[k]) for k in range(count)]
    for copy in copies:
        copy.start()
    for copy in copies:
        copy.wait()


def hand_out(*arrays):
    anywhere = pl.BlockSpec(memory_space=pl.ANY)
    return pl.pallas_call(
        hand_out_kernel,
        out_shape=[jax.ShapeDtypeStruct(a.shape, a.dtype) for a in arrays],
        in_specs=[anywhere] * len(arrays),
        out_specs=[pl.BlockSpec(memory_space=pltpu.HBM)] * len(arrays),
        scratch_shapes=[pltpu.SemaphoreType.DMA((len(arrays),))],
        compiler_params=pltpu.CompilerParams(vmem_limit_bytes=1 << 20),
        name="hand_out",
    )(*arrays)


def body(inputs, out_grads, weights, left_stats, right_stats, left_roots, right_roots, refresh):
    tok_local, model_width = inputs.shape
    block = weights.shape[1]
    col_count = out_grads.shape[1]
    row_blocks = model_width // block
    col_blocks = col_count // block
    replicas = lax.axis_size("dp")
    tok_total = tok_local * replicas
    kernels = col_blocks == 1 and row_blocks == replicas == 4 * LINE and lax.axis_size("owner") == 2 and block == 4 * tok_local
    rate = 0.25 / math.sqrt(model_width)
    if kernels:
        return hand_out(*fused_step(
            replicas, rate, inputs, out_grads, weights, left_stats, right_stats, left_roots, right_roots, refresh
        ))
    mine = lax.axis_index("dp") % col_blocks
    grads = lax.all_gather(out_grads, "dp", axis=0, tiled=True)
    grads = lax.dynamic_slice_in_dim(grads, mine * block, block, 1)
    send = jnp.repeat(inputs.reshape(tok_local, row_blocks, block).transpose(1, 0, 2), col_blocks, axis=0)
    features = lax.all_to_all(send, "dp", split_axis=0, concat_axis=0, tiled=True)
    features = features.reshape(tok_total, block)
    gradient = dot(features, grads, ((0,), (0,))) / tok_total
    left_new = BETA * left_stats[0] + (1.0 - BETA) * dot(gradient, gradient, ((1,), (1,)))
    right_new = BETA * right_stats[0] + (1.0 - BETA) * dot(gradient, gradient, ((0,), (0,)))
    left_root, right_root = lax.cond(
        refresh[0] > 0, roots, stale, left_new, right_new, left_roots[0], right_roots[0]
    )
    direction = dot3(dot3(left_root, gradient), right_root)
    direction = direction * (block / jnp.sqrt(jnp.sum(direction * direction) + 1e-12))
    updated = (weights[0] - rate * direction).astype(BF16)
    partial = dot(features, updated).astype(BF16)
    if col_blocks > 1:
        partial = lax.dynamic_update_slice(jnp.zeros((tok_total, col_count), BF16), partial, (0, mine * block))
    queries = lax.psum_scatter(partial, "dp", scatter_dimension=0, tiled=True)
    return (left_new[None], right_new[None], left_root[None], right_root[None], direction[None], queries)


def solution(mesh):
    blocks = P(("dp", "owner"), None, None)
    in_specs = (P("dp", None), P("dp", "owner"), blocks, blocks, blocks, blocks, blocks, P(("dp", "owner")))
    out_specs = (blocks,) * 5 + (P("dp", "owner"),)
    return jax.shard_map(body, mesh=mesh, in_specs=in_specs, out_specs=out_specs, check_vma=False)
```

```python
import functools
import math

import jax
import jax.numpy as jnp
from jax import lax
from jax.experimental import pallas as pl
from jax.experimental.pallas import tpu as pltpu
from jax.sharding import PartitionSpec as P

BETA = 0.95
DAMPING = 0.0001
BF16 = jnp.bfloat16
F32 = jnp.float32


def dot(a, b, dims=((1,), (0,))):
    return lax.dot_general(a.astype(BF16), b.astype(BF16), (dims, ((), ())), preferred_element_type=F32)


def split(a):
    high = a.astype(BF16)
    return high, (a - high.astype(F32)).astype(BF16)


def dot3(a, b):
    a_high, a_low = split(a)
    b_high, b_low = split(b)
    return dot(a_high, b_high) + (dot(a_high, b_low) + dot(a_low, b_high))


def even_dot(a, b, dims=((1,), (0,))):
    half = a.shape[0] // 2
    a, b = a.astype(BF16), b.astype(BF16)

    def cut(x, axis, low):
        return (x[:half] if low else x[half:]) if axis == 0 else (x[:, :half] if low else x[:, half:])

    over, under = (cut(a, 1 - dims[0][0], low) for low in (True, False))
    upper = dot(over, b, dims)
    corner = dot(under, cut(b, 1 - dims[1][0], False), dims)
    return jnp.concatenate([upper, jnp.concatenate([upper[:, half:].T, corner], axis=1)], axis=0)


def inverse_roots(*statistics):
    shape = statistics[0].shape
    eye = (lax.broadcasted_iota(jnp.int32, shape, 0) == lax.broadcasted_iota(jnp.int32, shape, 1)).astype(F32)
    damped = [s + DAMPING * eye for s in statistics]
    squares = [even_dot(a, a) for a in damped]
    z = [2.5 / jnp.sqrt(jnp.sum(a * a, keepdims=True)) for a in damped]
    m = [scale * a for scale, a in zip(z, damped)]
    p = [(scale * scale) * a for scale, a in zip(z, squares)]
    q = [even_dot(b, a) for a, b in zip(m, p)]
    r = [1.5625 * a - 0.625 * b + 0.0625 * c for a, b, c in zip(m, p, q)]
    w = [0.0625 * c + 0.1953125 * a - 0.01953125 * b for a, b, c in zip(m, p, r)]
    last = [even_dot(a, b) for a, b in zip(w, r)]
    return tuple(
        jnp.sqrt(jnp.sqrt(scale)) * (1.5625 * eye - 0.3125 * a - 0.48828125 * b + c)
        for scale, a, b, c in zip(z, m, r, last)
    )


def roots(left_stat, right_stat, left_old, right_old):
    return inverse_roots(left_stat, right_stat)


def stale(left_stat, right_stat, left_old, right_old):
    return (left_old, right_old)

LINE = 4


def flip(index, stride):
    return index + stride - 2 * stride * lax.rem(lax.div(index, stride), 2)


def remote(src, dst, send, recv, peer):
    return pltpu.make_async_remote_copy(
        src_ref=src, dst_ref=dst, send_sem=send, recv_sem=recv,
        device_id=peer, device_id_type=pl.DeviceIdType.MESH,
    )


def greet(peers):
    barrier = pltpu.get_barrier_semaphore()
    for peer in peers:
        pl.semaphore_signal(barrier, inc=1, device_id=peer, device_id_type=pl.DeviceIdType.MESH)
    pl.semaphore_wait(barrier, len(peers))


def toggle(index, bits):
    stride = 1
    while stride <= bits:
        if bits & stride:
            index = flip(index, stride)
        stride *= 2
    return index


ORDER = (
    "g", "x1", "x10", "x2", "x14", "x3", "x4", "h", "x6", "x11", "x15", "x5", "x8", "x7", "x12", "x9",
    "x13", "i1", "p1", "p2", "p4", "p10", "y0", "p3", "i3", "p14", "p6", "p11", "y2", "p15", "d0", "p5",
    "p7", "y1", "d2", "p8", "p12", "d10", "p9", "p13", "y3", "d14", "s3", "s11", "s15", "d6", "s7", "d4",
    "s5", "d8", "s9", "d12", "s13",
)


PARTS = {9: 2, 13: 2}
EXTRA = {(9, 1): 0, (13, 1): 16}


def landed(view, sem):
    pltpu.make_async_copy(view, view, sem).wait()


SPANS = 3
DIRECT = (0,)
HIGH = (
    "o3", "s3", "o1", "t3", "o2", "s2", "t1", "o0", "p30", "t2", "p31", "p32", "h", "s1", "s0", "t0",
    "p20", "p21", "p22", "g", "p10", "p11", "p12", "f", "q0", "q1", "q2",
)
LOW = (
    "o1", "s1", "o3", "s3", "t1", "o2", "t3", "o0", "p10", "t2", "p11", "p12", "s2", "h", "s0", "t0",
    "p30", "p31", "p32", "p20", "p21", "g", "p22", "f", "q0", "q1", "q2",
)


class Copies:
    def __init__(self, send):
        self.send = send

    def group(self, at):
        def go(src, dst, recv, peer):
            copy = remote(src, dst, self.send.at[at], recv, peer)
            copy.start()
            return copy

        return go


def gather_phase(n, copies, x_ref, g_ref, f, fs, ga, grad, own, x_r, p_r, z_r, y_r, c_r, s_r):
    me, mine = lax.axis_index("dp"), lax.axis_index("owner")
    rows, width = g_ref.shape
    half = rows // 2
    far = pl.ds(pl.multiple_of((1 - mine) * half, half), half)
    pair, row = flip(me, 1), flip(me, 2)
    go_x, go_g, go_s = copies.group(0), copies.group(1), copies.group(2)

    def cols(block):
        return pl.ds(pl.multiple_of(block * width, width), width)

    own_in = [
        pltpu.make_async_copy(x_ref.at[:, cols(me)], f.at[me], own.at[0]),
        pltpu.make_async_copy(g_ref, ga.at[me], own.at[1]),
        pltpu.make_async_copy(x_ref.at[:, cols(pair)], fs.at[lax.div(me, 2)], own.at[2]),
    ]
    x_copy, z_copy, y_copy, c_copy = {}, {}, {}, {}

    def fan(t, block):
        slot = toggle(me, LINE * t)
        y_copy[t] = go_g(block, ga.at[slot], y_r.at[t], (row, mine))
        c_copy[t] = go_g(block, ga.at[slot], c_r.at[t], (pair, mine))

    def g(_):
        for copy in own_in:
            copy.start()
        for t in (2, 1):
            z_copy[t] = go_g(g_ref, ga.at[me], z_r.at[t], (toggle(me, LINE * t), mine))
        fan(0, g_ref)

    def h(_):
        z_copy[2].wait_recv()
        held = ga.at[toggle(me, LINE * 2)]
        z_copy[3] = go_g(held, held, z_r.at[3], (toggle(me, LINE), mine))
        fan(2, held)

    def i(t):
        z_copy[t].wait_recv()
        fan(t, ga.at[toggle(me, LINE * t)])

    def y(t):
        y_copy[t].wait_recv()
        held = ga.at[toggle(row, LINE * t)]
        c_copy[LINE + t] = go_g(held, held, c_r.at[LINE + t], (pair, mine))

    def slices(k):
        count = PARTS.get(k, 1)
        span = half // count
        return [pl.ds(pl.multiple_of(mine * half + at * span, span), span) for at in range(count)]

    def x(k):
        peer = toggle(me, k)
        if k == 1:
            x_copy[k] = [go_x(x_ref.at[:, cols(peer)], f.at[me], x_r.at[k], (peer, mine))]
            return
        x_copy[k] = []
        for at, part in enumerate(slices(k)):
            sem = x_r.at[k if at == 0 else EXTRA[k, at]]
            x_copy[k].append(go_x(x_ref.at[part, cols(peer)], f.at[me, part], sem, (peer, mine)))

    def p(k):
        if k == 1:
            x_copy[k][0].wait_recv()
            return
        for at, part in enumerate(slices(k)):
            x_copy[k][at].wait_recv()
            held = f.at[toggle(me, k), part]
            go_x(held, held, p_r.at[k // 2], (me, 1 - mine))

    def d(k):
        chip = pl.ds(pl.multiple_of(2 * lax.div(toggle(me, k), 2), 2), 2)
        if k:
            landed(f.at[chip, far], p_r.at[k // 2])
        else:
            own_in[0].wait()
            own_in[1].wait()
        t = k // LINE
        c_copy[t + LINE if k % LINE else t].wait_recv()
        term = dot(f[chip].reshape(2 * rows, width), ga[chip].reshape(2 * rows, width), ((0,), (0,)))
        grad[...] = term if k == 0 else grad[...] + term

    def s(k):
        source = toggle(me, k)
        go_s(f.at[source], fs.at[lax.div(source, 2)], s_r.at[0], (pair, mine))

    steps = dict(g=g, h=h, i=i, y=y, x=x, p=p, d=d, s=s)
    for word in ORDER:
        with jax.named_scope(word):
            steps[word[0]](int(word[1:] or 0))
    return own_in[2]


def reduce_phase(order, copies, feats, fs, u, us, arrive, q, tot, ahead, keep, a_out, a_in, b_out, b_in, e_out, e_in, h_out, h_in, g_out, g_in,
                 a_r, b_r, e_r):
    me, mine = lax.axis_index("dp"), lax.axis_index("owner")
    row = flip(me, 2)
    rows = q.shape[0]
    cut = rows // 4
    third = (rows - cut) // SPANS
    go = copies.group(3)
    first = pl.ds(0, cut)
    rest = [pl.ds(cut + k * third, third) for k in range(SPANS)]
    spans = [pl.ds(k * third, third) for k in range(SPANS)]
    near_z, far_z, direct, across = (toggle(me, LINE), mine), (toggle(me, 2 * LINE), mine), (toggle(me, 3 * LINE), mine), (row, mine)

    def near_part(base, t):
        return dot(feats[toggle(base, LINE * t)], u[...])

    def far_part(base, t):
        return dot(fs[lax.div(toggle(base, LINE * t), 2)], us[...])

    a_copy, b_copy, h_copy, g_copy = {}, {}, [], []
    for t in range(LINE):
        ahead[t] = near_part(row, t)
    with jax.named_scope("swap"):
        arrive()

    def o(t):
        value = ahead[t] + far_part(row, t)
        a_out[t] = value[cut:].astype(BF16)
        if t % 2:
            early(0 if t == 3 else 1, value)
        else:
            keep[0 if t == 2 else 1] = value[:cut]

    def t(t):
        value = near_part(me, t) + far_part(me, t)
        if t % 2:
            early(2 if t == 3 else 3, value)
        tot[t] = value

    def early(k, value):
        e_out[k] = value[:cut].astype(BF16)
        go(e_out.at[k], e_in.at[k], e_r.at[k // 2], near_z)

    def s(t):
        for k in range(SPANS):
            a_copy[t, k] = go(a_out.at[t, spans[k]], a_in.at[t, spans[k]], a_r.at[SPANS * t + k], across)

    def p(t, k):
        a_copy[t, k].wait_recv()
        value = tot[t, rest[k]] + a_in[t, spans[k]].astype(F32)
        peer = near_z
        if t == 2:
            peer = far_z
            if k not in DIRECT:
                b_copy[3, k].wait_recv()
                value = value + b_in[3, spans[k]].astype(F32)
        elif t == 3 and k in DIRECT:
            peer = direct
        b_out[t, spans[k]] = value.astype(BF16)
        b_copy[t, k] = go(b_out.at[t, spans[k]], b_in.at[t, spans[k]], b_r.at[SPANS * t + k], peer)

    def h():
        landed(e_in.at[pl.ds(0, 2)], e_r.at[0])
        for k in range(2):
            h_out[k] = (keep[k] + e_in[k].astype(F32)).astype(BF16)
            h_copy.append(go(h_out.at[k], h_in.at[k], e_r.at[3 + k], across))

    def g():
        landed(e_in.at[pl.ds(2, 2)], e_r.at[1])
        h_copy[0].wait_recv()
        g_out[...] = (tot[2, first] + e_in[2].astype(F32) + h_in[0].astype(F32)).astype(BF16)
        g_copy.append(go(g_out, g_in, e_r.at[2], far_z))

    def f():
        h_copy[1].wait_recv()
        g_copy[0].wait_recv()
        q[first] = (tot[0, first] + e_in[3].astype(F32) + h_in[1].astype(F32) + g_in[...].astype(F32)).astype(BF16)

    def q_(k):
        a_copy[0, k].wait_recv()
        value = tot[0, rest[k]] + a_in[0, spans[k]].astype(F32)
        for at in (3, 2, 1) if k in DIRECT else (2, 1):
            b_copy[at, k].wait_recv()
            value = value + b_in[at, spans[k]].astype(F32)
        q[rest[k]] = value.astype(BF16)

    steps = dict(o=o, t=t, s=s, p=p, h=h, g=g, f=f, q=q_)
    for word in order:
        with jax.named_scope("r" + word):
            steps[word[0]](*map(int, word[1:]))


def step_kernel(n, rate, flag, x_ref, g_ref, w_hbm, ls_hbm, rs_hbm, lr_hbm, rr_hbm,
                ls_out, rs_out, lr_out, rr_out, d_out, q_ref,
                f, fs, ga, grad, w, ls, rs, lr, rr, d, u, us, q, tot, ahead, keep, a_out, a_in, b_out, b_in, e_out, e_in, h_out, h_in, g_out, g_in,
                in_sem, out_sem, send, own, x_r, p_r, z_r, y_r, c_r, s_r, u_r, a_r, b_r, e_r):
    me, mine = lax.axis_index("dp"), lax.axis_index("owner")
    pair = flip(me, 1)
    block = w.shape[0]
    with jax.named_scope("greet"):
        greet([(toggle(me, k), mine) for k in range(1, n)] + [(me, 1 - mine)])
    copies = Copies(send)
    ins = [
        pltpu.make_async_copy(src.at[0], dst, in_sem.at[k])
        for k, (src, dst) in enumerate(((ls_hbm, ls), (rs_hbm, rs), (lr_hbm, lr), (rr_hbm, rr), (w_hbm, w)))
    ]
    for copy in ins:
        copy.start()
    own_side = gather_phase(n, copies, x_ref, g_ref, f, fs, ga, grad, own, x_r, p_r, z_r, y_r, c_r, s_r)
    outs = [
        pltpu.make_async_copy(src, dst.at[0], out_sem.at[k])
        for k, (src, dst) in enumerate(((ls, ls_out), (rs, rs_out), (lr, lr_out), (rr, rr_out), (d, d_out)))
    ]
    with jax.named_scope("stats"):
        for copy in ins:
            copy.wait()
        high = (grad[...] * (1.0 / (n * g_ref.shape[0]))).astype(BF16)
        ls[...] = BETA * ls[...] + (1.0 - BETA) * even_dot(high, high, ((1,), (1,)))
        rs[...] = BETA * rs[...] + (1.0 - BETA) * even_dot(high, high, ((0,), (0,)))
        outs[0].start()
        outs[1].start()
    with jax.named_scope("roots"):
        anew = jnp.full((block, block), flag[0], jnp.int32) > 0
        left, right = inverse_roots(ls[...], rs[...])
        lr[...] = jnp.where(anew, left, lr[...])
        rr[...] = jnp.where(anew, right, rr[...])
        outs[2].start()
        outs[3].start()
    with jax.named_scope("direction"):
        through = dot(lr[...], high).astype(BF16)
        last = rr[...].astype(BF16)
        total = jnp.zeros((8, block), F32)
        for k in range(4):
            span = block // 4
            value = dot(through[k * span : (k + 1) * span], last)
            d[pl.ds(k * span, span)] = value
            total = total + jnp.sum((value * value).reshape(span // 8, 8, block), axis=0)
    with jax.named_scope("update"):
        scale = block / jnp.sqrt(jnp.sum(total, keepdims=True) + 1e-12)
    for k in range(2):
        with jax.named_scope(f"weights{k}"):
            part = pl.ds(k * block // 2, block // 2)
            u[part] = (w[part] - (rate * scale) * d[part]).astype(BF16)
            copies.group(2)(u.at[part], us.at[part], u_r.at[0], (pair, mine))
    with jax.named_scope("scaled"):
        d[...] = scale * d[...]
        outs[4].start()

    def arrive():
        own_side.wait()
        landed(fs.at[pl.ds(0, n // 2 - 1)], s_r.at[0])
        landed(us, u_r.at[0])

    def reduce_in(order):
        reduce_phase(
            order, copies, f, fs, u, us, arrive, q, tot, ahead, keep,
            a_out, a_in, b_out, b_in, e_out, e_in, h_out, h_in, g_out, g_in, a_r, b_r, e_r,
        )

    low = lax.div(me, LINE) < LINE // 2
    pl.when(low)(functools.partial(reduce_in, LOW))
    pl.when(jnp.logical_not(low))(functools.partial(reduce_in, HIGH))
    with jax.named_scope("drain"):
        q_out = pltpu.make_async_copy(q, q_ref, out_sem.at[5])
        q_out.start()
        q_out.wait()
        for copy in outs:
            copy.wait()
        for at, units in enumerate((n - 1, n - 1, n // 2 + 3, n // 2 - 1)):
            landed(f.at[pl.ds(0, units)], send.at[at])


def fused_step(n, rate, inputs, out_grads, weights, left_stats, right_stats, left_roots, right_roots, refresh):
    rows, width = out_grads.shape
    block = weights.shape[1]
    nz = n // LINE
    dma = pltpu.SemaphoreType.DMA
    anywhere = pl.BlockSpec(memory_space=pl.ANY)
    square = pltpu.VMEM((block, block), F32)
    narrow = pltpu.VMEM((block, block), BF16)
    cut = rows // 4
    shards = pltpu.VMEM((nz, rows - cut, width), BF16)
    return pl.pallas_call(
        functools.partial(step_kernel, n, rate),
        out_shape=[jax.ShapeDtypeStruct((1, block, block), F32)] * 5 + [jax.ShapeDtypeStruct((rows, width), BF16)],
        in_specs=[pl.BlockSpec(memory_space=pltpu.SMEM)] + [pl.BlockSpec(memory_space=pltpu.HBM)] * 7,
        out_specs=[anywhere] * 6,
        scratch_shapes=[
            pltpu.VMEM((n, rows, block), BF16), pltpu.VMEM((n // 2, rows, block), BF16), pltpu.VMEM((n, rows, width), BF16),
        ] + [square] * 7 + [narrow] * 2 + [pltpu.VMEM((rows, width), BF16)] + [pltpu.VMEM((nz, rows, width), F32)] * 2 + [pltpu.VMEM((2, cut, width), F32)] + [shards] * 4
        + [pltpu.VMEM((4, cut, width), BF16)] * 2 + [pltpu.VMEM((2, cut, width), BF16)] * 2 + [pltpu.VMEM((cut, width), BF16)] * 2
        + [dma((5,)), dma((6,)), dma((4,)), dma((3,))]
        + [dma((n + len(EXTRA) - 1,)), dma((n // 2,)), dma((LINE,)), dma((LINE,)), dma((2 * LINE,)), dma((1,)), dma((1,))]
        + [dma((SPANS * LINE,)), dma((SPANS * LINE,)), dma((5,))],
        compiler_params=pltpu.CompilerParams(collective_id=0, has_side_effects=True, vmem_limit_bytes=48 << 20),
        name="fused_step",
    )(refresh, inputs, pltpu.with_memory_space_constraint(out_grads, pltpu.HBM), weights, left_stats, right_stats, left_roots, right_roots)


def hand_out_kernel(*refs):
    count = len(refs) // 2
    copies = [pltpu.make_async_copy(refs[k], refs[count + k], refs[-1].at[k]) for k in range(count)]
    for copy in copies:
        copy.start()
    for copy in copies:
        copy.wait()


def hand_out(*arrays):
    anywhere = pl.BlockSpec(memory_space=pl.ANY)
    return pl.pallas_call(
        hand_out_kernel,
        out_shape=[jax.ShapeDtypeStruct(a.shape, a.dtype) for a in arrays],
        in_specs=[anywhere] * len(arrays),
        out_specs=[pl.BlockSpec(memory_space=pltpu.HBM)] * len(arrays),
        scratch_shapes=[pltpu.SemaphoreType.DMA((len(arrays),))],
        compiler_params=pltpu.CompilerParams(vmem_limit_bytes=1 << 20),
        name="hand_out",
    )(*arrays)


def body(inputs, out_grads, weights, left_stats, right_stats, left_roots, right_roots, refresh):
    tok_local, model_width = inputs.shape
    block = weights.shape[1]
    col_count = out_grads.shape[1]
    row_blocks = model_width // block
    col_blocks = col_count // block
    replicas = lax.axis_size("dp")
    tok_total = tok_local * replicas
    kernels = col_blocks == 1 and row_blocks == replicas == 4 * LINE and lax.axis_size("owner") == 2 and block == 4 * tok_local
    rate = 0.25 / math.sqrt(model_width)
    if kernels:
        return hand_out(*fused_step(
            replicas, rate, inputs, out_grads, weights, left_stats, right_stats, left_roots, right_roots, refresh
        ))
    mine = lax.axis_index("dp") % col_blocks
    grads = lax.all_gather(out_grads, "dp", axis=0, tiled=True)
    grads = lax.dynamic_slice_in_dim(grads, mine * block, block, 1)
    send = jnp.repeat(inputs.reshape(tok_local, row_blocks, block).transpose(1, 0, 2), col_blocks, axis=0)
    features = lax.all_to_all(send, "dp", split_axis=0, concat_axis=0, tiled=True)
    features = features.reshape(tok_total, block)
    gradient = dot(features, grads, ((0,), (0,))) / tok_total
    left_new = BETA * left_stats[0] + (1.0 - BETA) * dot(gradient, gradient, ((1,), (1,)))
    right_new = BETA * right_stats[0] + (1.0 - BETA) * dot(gradient, gradient, ((0,), (0,)))
    left_root, right_root = lax.cond(
        refresh[0] > 0, roots, stale, left_new, right_new, left_roots[0], right_roots[0]
    )
    direction = dot3(dot3(left_root, gradient), right_root)
    direction = direction * (block / jnp.sqrt(jnp.sum(direction * direction) + 1e-12))
    updated = (weights[0] - rate * direction).astype(BF16)
    partial = dot(features, updated).astype(BF16)
    if col_blocks > 1:
        partial = lax.dynamic_update_slice(jnp.zeros((tok_total, col_count), BF16), partial, (0, mine * block))
    queries = lax.psum_scatter(partial, "dp", scatter_dimension=0, tiled=True)
    return (left_new[None], right_new[None], left_root[None], right_root[None], direction[None], queries)


def solution(mesh):
    blocks = P(("dp", "owner"), None, None)
    in_specs = (P("dp", None), P("dp", "owner"), blocks, blocks, blocks, blocks, blocks, P(("dp", "owner")))
    out_specs = (blocks,) * 5 + (P("dp", "owner"),)
    return jax.shard_map(body, mesh=mesh, in_specs=in_specs, out_specs=out_specs, check_vma=False)
```
